32 devices in a mesh: grp: 2 (over y), patch: 8 (over z, x), frame: 2 (over core).
Axes of the slice: x: 2, y: 2, z: 4, core: 2. Of those that a mesh axis runs over, the one named last changes fastest.
Arguments:
- video_tokens: bfloat16 [4, 16, 80, 1152], P('grp', 'frame', 'patch'), parts along dimension 0, may hold values from -6 to 6
- timestep: int32 [2], P('grp'), parts along dimension 0, may hold values from 0 to 999
- w_qkv: bfloat16 [2, 1152, 1728], P(None, 'patch'), may hold values from -0.1875 to 0.1875
- w_out: bfloat16 [2, 576, 1152], P(None, None, 'patch'), may hold values from -0.25 to 0.25
- qk_gain: float32 [2, 2, 72], replicated, may hold values from 1 to 2.5
- mod_table: float32 [2, 3, 1152], replicated, may hold values from -3 to 3
- mod_gain: float32 [2, 3, 1152], replicated, may hold values from -3 to 3
Outputs:
- denoised: bfloat16 [4, 16, 80, 1152], P('grp', 'frame', 'patch'), parts along dimension 0
The draws below stay inside these ranges and needn't reach their ends.
There are 2 independent parts, one for each index of `grp`. The reference program is written for one: setup_inputs(seed, part) draws one part's arguments, and reference() takes and returns one part's arrays. A program takes and returns all parts, laid end to end along the dimension named above; an argument that names none is the same for every part. Nothing has to cross between parts.
All inputs are finite; a program needn't handle non-finite values.
Results may differ from the reference program's by a relative error of at most 0.013.
Values may be sent and summed in bfloat16 or wider, within the bound.
A program may use at most 128 MiB of HBM per device.

```python
import math
import jax
import jax.numpy as jnp
from jax import lax

D = 1152
HEAD_DIM = 72
HEADS = 8
LAYERS = 2
VIDEOS = 2
FRAMES = 16
PATCHES = 80


def block_scale(key, shape, shards, smallest, high):
    def one(dim, shards_of):
        heights = jax.random.uniform(jax.random.fold_in(jax.random.fold_in(key, 6), dim), (shards_of,), jnp.float32, smallest / len(shards), high / len(shards))
        return jnp.repeat(jnp.exp(heights), shape[dim] // shards_of).reshape((-1,) + (1,) * (len(shape) - dim - 1))

    level = one(*shards[0])
    for cut in shards[1:]:
        level = level * one(*cut)
    return level


def gaussian(own_key, extent, scale, limit, shards=(), kind=jnp.bfloat16):
    array = jax.random.normal(own_key, extent, jnp.float32) * scale
    if len(shards) > 0:
        array = block_scale(own_key, extent, shards, -0.22, 0.18) * array
    return jnp.clip(array, min=-limit, max=limit).astype(kind)


def setup_inputs(seed: int = 0, part: int = 0) -> dict:
    arg_keys = jax.random.split(jax.random.key(seed), 8)
    part_keys = jax.random.split(jax.random.fold_in(arg_keys[7], part), 8)
    return {
        "video_tokens": gaussian(part_keys[0], (VIDEOS, FRAMES, PATCHES, D), 1.0, 6.0, ((1, 2), (2, 8))),
        "timestep": jax.random.randint(part_keys[1], (1,), 0, 1000).astype(jnp.int32),
        "w_qkv": gaussian(arg_keys[2], (LAYERS, D, 3 * HEADS * HEAD_DIM), D ** -0.5, 0.1875, ((1, 8),)),
        "w_out": gaussian(arg_keys[3], (LAYERS, HEADS * HEAD_DIM, D), (HEADS * HEAD_DIM) ** -0.5, 0.25, ((2, 8),)),
        "qk_gain": jnp.clip(jnp.exp(jax.random.uniform(arg_keys[4], (LAYERS, 2, HEAD_DIM), jnp.float32, math.log(1.0), math.log(2.5))), 1.0, 2.5),
        "mod_table": gaussian(arg_keys[5], (LAYERS, 3, D), 0.5, 3.0, (), jnp.float32),
        "mod_gain": gaussian(arg_keys[6], (LAYERS, 3, D), 0.5, 3.0, (), jnp.float32),
    }


def time_embed(timestep, width):
    half_width = width // 2
    freqs = jnp.exp(-math.log(10000.0) * jnp.arange(half_width, dtype=jnp.float32) / half_width)
    angles = timestep[0].astype(jnp.float32) * freqs
    return jnp.concatenate([jnp.cos(angles), jnp.sin(angles)])

def modulate(tokens, table, gains, embed):
    params = table + gains * embed[None, :]
    values = tokens.astype(jnp.float32)
    centre = lax.optimization_barrier(jnp.mean(values, axis=-1, keepdims=True))
    centred = values - centre
    spread = lax.optimization_barrier(jnp.mean(centred * centred, axis=-1, keepdims=True))
    normed = centred * lax.rsqrt(spread + 1e-06)
    return ((normed * (1.0 + params[1]) + params[0]).astype(jnp.bfloat16), params[2])

def head_norm(values, gain):
    meansq = lax.optimization_barrier(jnp.mean(values * values, axis=-1, keepdims=True))
    return (values * lax.rsqrt(meansq + 1e-06) * gain).astype(jnp.bfloat16)

def attend(query, key, value):
    scores = jnp.einsum('nqd,nkd->nqk', query.astype(jnp.float32), key.astype(jnp.float32)) / math.sqrt(HEAD_DIM)
    raised = jnp.exp(scores)
    total = lax.optimization_barrier(jnp.sum(raised, axis=-1, keepdims=True))
    weights = lax.optimization_barrier(raised.astype(jnp.bfloat16)).astype(jnp.float32)
    summed = jnp.einsum('nqk,nkd->nqd', weights, value.astype(jnp.float32))
    return (summed / total).astype(jnp.bfloat16)

def reference(video_tokens, timestep, w_qkv, w_out, qk_gain, mod_table, mod_gain):
    videos, frames, patches, width = video_tokens.shape
    rows = videos * frames * patches
    feat = HEADS * HEAD_DIM
    embed = time_embed(timestep, width)
    tokens = video_tokens.reshape(rows, width)
    for layer in range(2):
        mixed, gate = modulate(tokens, mod_table[layer], mod_gain[layer], embed)
        joint = jnp.dot(mixed, w_qkv[layer], preferred_element_type=jnp.float32)
        joint = joint.reshape(rows, 3, HEADS, HEAD_DIM)
        query = head_norm(joint[:, 0], qk_gain[layer, 0])
        key = head_norm(joint[:, 1], qk_gain[layer, 1])
        value = joint[:, 2].astype(jnp.bfloat16)
        shape5 = (videos, frames, patches, HEADS, HEAD_DIM)
        if layer == 0:

            def items(arr):
                return arr.reshape(shape5).transpose(0, 1, 3, 2, 4).reshape(videos * frames, HEADS, patches, HEAD_DIM)
            result = lax.map(lambda trio: attend(trio[0], trio[1], trio[2]), (items(query), items(key), items(value)))
            attended = result.reshape(videos, frames, HEADS, patches, HEAD_DIM).transpose(0, 1, 3, 2, 4).reshape(rows, feat)
        else:

            def items(arr):
                return arr.reshape(shape5).transpose(0, 2, 3, 1, 4).reshape(videos * patches * HEADS, frames, HEAD_DIM)
            result = attend(items(query), items(key), items(value))
            attended = result.reshape(videos, patches, HEADS, frames, HEAD_DIM).transpose(0, 3, 1, 2, 4).reshape(rows, feat)
        update = jnp.dot(attended, w_out[layer], preferred_element_type=jnp.float32)
        tokens = (tokens.astype(jnp.float32) + gate * update).astype(jnp.bfloat16)
    return tokens.reshape(videos, frames, patches, width)
```

```python
import functools
import math

import jax
import jax.numpy as jnp
import numpy as np
from jax import lax
from jax.experimental import pallas as pl
from jax.experimental.pallas import tpu as pltpu
from jax.sharding import PartitionSpec as P


def time_embed(timestep, width):
    half_width = width // 2
    freqs = jnp.exp(-math.log(10000.0) * jnp.arange(half_width, dtype=jnp.float32) / half_width)
    angles = timestep[0].astype(jnp.float32) * freqs
    return jnp.concatenate([jnp.cos(angles), jnp.sin(angles)])


def modulate(tokens, table, gains, embed):
    params = table + gains * embed[None, :]
    values = tokens.astype(jnp.float32)
    centre = jnp.mean(values, axis=-1, keepdims=True)
    centred = values - centre
    spread = jnp.mean(centred * centred, axis=-1, keepdims=True)
    normed = centred * lax.rsqrt(spread + 1e-06)
    return ((normed * (1.0 + params[1]) + params[0]).astype(jnp.bfloat16), params[2])


def head_norm(values, gain):
    meansq = jnp.mean(values * values, axis=-1, keepdims=True)
    return (values * lax.rsqrt(meansq + 1e-06) * gain).astype(jnp.bfloat16)


def fetch_weights(qkv_rows, out_cols):
    return (
        lax.all_gather(qkv_rows, "patch", axis=0, tiled=True),
        lax.all_gather(out_cols, "patch", axis=1, tiled=True),
    )


def attend_items(stacked):
    head_size = stacked.shape[-1]
    query = stacked[0, 0]
    key = stacked[1, 0]
    value = stacked[2, 0]
    scores = jnp.einsum("nqd,nkd->nqk", query, key, preferred_element_type=jnp.float32) / math.sqrt(
        head_size
    )
    raised = jnp.exp(scores)
    total = jnp.sum(raised, axis=-1, keepdims=True)
    summed = jnp.einsum(
        "nqk,nkd->nqd", raised.astype(jnp.bfloat16), value, preferred_element_type=jnp.float32
    )
    return (summed / total).astype(jnp.bfloat16)[None]


def spatial(query, key, value, videos, fr_dev, patch_dev):
    rows, heads, head_size = query.shape
    groups = lax.axis_size("patch")
    per_group = videos * fr_dev * heads // groups
    stacked = jnp.stack([query, key, value])
    stacked = stacked.reshape(3, videos * fr_dev, patch_dev, heads, head_size)
    stacked = stacked.transpose(0, 1, 3, 2, 4).reshape(3, groups, per_group, patch_dev, head_size)
    attended = attend_items(
        lax.all_to_all(stacked, "patch", split_axis=1, concat_axis=3, tiled=True)
    )
    returned = lax.all_to_all(attended, "patch", split_axis=2, concat_axis=0, tiled=True)
    returned = returned.reshape(videos * fr_dev, heads, patch_dev, head_size).transpose(0, 2, 1, 3)
    return returned.reshape(rows, heads * head_size)


def frame_attend(query, key, value, heads):
    videos, q_frames, patches, feat = query.shape
    k_frames = key.shape[1]
    head_size = feat // heads
    query = query.reshape(videos, q_frames, patches, heads, head_size)
    key = key.reshape(videos, k_frames, patches, heads, head_size)
    value = value.reshape(videos, k_frames, patches, heads, head_size)
    scores = jnp.einsum(
        "bfphd,bgphd->bphfg", query, key, preferred_element_type=jnp.float32
    ) / math.sqrt(head_size)
    raised = jnp.exp(scores)
    total = jnp.sum(raised, axis=-1)
    summed = jnp.einsum(
        "bphfg,bgphd->bfphd", raised.astype(jnp.bfloat16), value, preferred_element_type=jnp.float32
    )
    result = summed / total.transpose(0, 3, 1, 2)[..., None]
    return result.astype(jnp.bfloat16).reshape(videos, q_frames, patches, feat)


def temporal(query, key, value, videos, fr_dev, patch_dev):
    rows, heads, head_size = query.shape
    feat = heads * head_size
    query4 = query.reshape(videos, fr_dev, patch_dev, feat)
    key4 = key.reshape(videos, fr_dev, patch_dev, feat)
    value4 = value.reshape(videos, fr_dev, patch_dev, feat)
    joined = jnp.concatenate([query4, key4, value4], axis=3)
    swapped = lax.all_to_all(joined, "frame", split_axis=2, concat_axis=1, tiled=True)
    result = frame_attend(
        swapped[..., :feat], swapped[..., feat : 2 * feat], swapped[..., 2 * feat :], heads
    )
    returned = lax.all_to_all(result, "frame", split_axis=1, concat_axis=2, tiled=True)
    return returned.reshape(rows, feat)


def per_device(video_tokens, timestep, w_qkv, w_out, qk_gain, mod_table, mod_gain):
    videos, fr_dev, patch_dev, width = video_tokens.shape
    rows = videos * fr_dev * patch_dev
    head_size = qk_gain.shape[2]
    heads = w_out.shape[1] // head_size
    embed = time_embed(timestep, width)
    tokens = video_tokens.reshape(rows, width)
    for layer in range(2):
        qkv_full, out_full = fetch_weights(w_qkv[layer], w_out[layer])
        mixed, gate = modulate(tokens, mod_table[layer], mod_gain[layer], embed)
        joint = jnp.dot(mixed, qkv_full, preferred_element_type=jnp.float32)
        joint = joint.reshape(rows, 3, heads, head_size)
        query = head_norm(joint[:, 0], qk_gain[layer, 0])
        key = head_norm(joint[:, 1], qk_gain[layer, 1])
        value = joint[:, 2].astype(jnp.bfloat16)
        if layer == 0:
            attended = spatial(query, key, value, videos, fr_dev, patch_dev)
        else:
            attended = temporal(query, key, value, videos, fr_dev, patch_dev)
        update = jnp.dot(attended, out_full, preferred_element_type=jnp.float32)
        tokens = (tokens.astype(jnp.float32) + gate * update).astype(jnp.bfloat16)
    return tokens.reshape(videos, fr_dev, patch_dev, width)


MESH = pl.DeviceIdType.MESH
HIGHEST = lax.Precision.HIGHEST


def dot_f32(a, b, contract):
    return lax.dot_general(
        a, b, ((contract[:1], contract[1:]), ((), ())), preferred_element_type=jnp.float32
    )


def dot_exact(a, b, contract):
    return lax.dot_general(
        a,
        b,
        ((contract[:1], contract[1:]), ((), ())),
        precision=HIGHEST,
        preferred_element_type=jnp.float32,
    )


def norm_tokens(values, params):
    centre = jnp.mean(values, axis=-1, keepdims=True)
    centred = values - centre
    spread = jnp.mean(centred * centred, axis=-1, keepdims=True)
    normed = centred * lax.rsqrt(spread + 1e-06)
    return (normed * (1.0 + params[1]) + params[0]).astype(jnp.bfloat16)


def norm_heads(values, gain, heads_map, head_size):
    total = dot_exact(values * values, heads_map, (1, 1))
    scale = lax.rsqrt(total / head_size + 1e-06)
    wide = dot_exact(scale, heads_map, (1, 0))
    return (values * wide * gain).astype(jnp.bfloat16)


def attend_heads(query, key, value, heads_map, mask, att_ref, head_size, between):
    feat = query.shape[1]
    att_ref[...] = jnp.zeros_like(att_ref)
    for head in range(feat // head_size):
        low = head * head_size // 128 * 128
        high = min(-(-(head + 1) * head_size // 128) * 128, feat)
        lanes = heads_map[head : head + 1, low:high].astype(jnp.bfloat16)
        scores = dot_f32(query[:, low:high] * lanes, key[:, low:high], (1, 1))
        raised = jnp.where(mask, jnp.exp(scores / math.sqrt(head_size)), 0.0)
        total = jnp.sum(raised, axis=-1, keepdims=True)
        summed = dot_f32(raised.astype(jnp.bfloat16), value[:, low:high] * lanes, (1, 0))
        att_ref[:, low:high] += summed / total
        between(head)
    return att_ref[...].astype(jnp.bfloat16)


def iota(shape, dim):
    return lax.broadcasted_iota(jnp.int32, shape, dim)


def fused_kernel(
    head_size, emb_ref, gain_ref, tab_ref, mgain_ref, x_hbm, wq_hbm, wo_hbm, out_ref,
    wbuf, stage_q, stage_o, stage_x, xsend, xin, mid_send, mid_recv, xf, att, res,
    local_sem, ici_send, ici_recv, sib_send, sib_recv,
    in_send, in_recv, mid_ssem, mid_rsem, fin_send, fin_recv,
):
    videos, patch_dev, fr_dev, width = x_hbm.shape
    layers, rows, _ = wq_hbm.shape
    feat = wo_hbm.shape[2]
    heads = feat // head_size
    count = fr_dev
    tokens = videos * patch_dev * fr_dev
    half = wbuf.shape[2] // 2
    grp = lax.axis_index("grp")
    me = lax.axis_index("patch")
    core = lax.axis_index("frame")
    sib = 1 - core
    level, side = lax.div(me, 2), lax.rem(me, 2)
    across = level * 2 + 1 - side
    zlen = -(-rows // 32) * 16
    ylen = rows - zlen

    stage = [
        pltpu.make_async_copy(wq_hbm, stage_q, local_sem.at[0]),
        pltpu.make_async_copy(wo_hbm, stage_o, local_sem.at[1]),
        pltpu.make_async_copy(x_hbm, stage_x, local_sem.at[2]),
    ]
    for copy in stage:
        copy.start()

    barrier = pltpu.get_barrier_semaphore()
    for k in range(count):
        for s in range(2):
            if k or s:
                pl.semaphore_signal(
                    barrier,
                    inc=1,
                    device_id=(grp, lax.rem(me + k, count), lax.rem(core + s, 2)),
                    device_id_type=MESH,
                )
    pl.semaphore_signal(
        barrier, inc=1, device_id=(1 - grp, me, core), device_id_type=MESH
    )

    def remote(src, dst, send_sem, recv_sem, patch, frame, to_grp=grp):
        return pltpu.make_async_remote_copy(
            src_ref=src,
            dst_ref=dst,
            send_sem=send_sem,
            recv_sem=recv_sem,
            device_id=(to_grp, patch, frame),
            device_id_type=MESH,
        )

    def block(layer, shard, start, size, of=core):
        first = pl.multiple_of(shard * rows + start, 16)
        return wbuf.at[
            layer, pl.ds(first, size), pl.ds(pl.multiple_of(of * half, 128), half)
        ]

    def copy_to(layer, shard, start, size, slot, patch, to_grp):
        part = block(layer, shard, start, size)
        return remote(
            part, part, ici_send.at[layer], ici_recv.at[layer, slot], patch, core, to_grp
        )

    def to_sibling(layer, shard, start, size):
        part = block(layer, shard, start, size)
        remote(part, part, sib_send.at[layer], sib_recv.at[layer], me, sib).start()

    def level_of(j):
        step = j + 1
        low, high = lax.rem(level, 2), lax.div(level, 2)
        low = low + (step % 2) * (1 - 2 * low)
        high = high + (step // 2) * (1 - 2 * high)
        return high * 2 + low

    mine, give, lack = grp * (rows - zlen), grp * zlen, (1 - grp) * zlen

    def send_own(layer):
        for j in range(3):
            copy_to(layer, me, mine, zlen, j, level_of(j) * 2 + side, grp).start()
        copy_to(layer, me, 0, rows, 3, across, grp).start()

    def landed_z(layer, j):
        shard = level_of(j) * 2 + side
        copy_to(layer, shard, mine, zlen, j, me, grp).wait_recv()
        copy_to(layer, shard, mine, zlen, 4 + j, across, grp).start()
        copy_to(layer, shard, give, ylen, 7 + j, me, 1 - grp).start()
        to_sibling(layer, shard, mine, zlen)

    def landed_own(layer):
        copy_to(layer, across, 0, rows, 3, me, grp).wait_recv()
        to_sibling(layer, across, 0, rows)

    def landed_x(layer, j):
        shard = level_of(j) * 2 + 1 - side
        copy_to(layer, shard, mine, zlen, 4 + j, me, grp).wait_recv()
        copy_to(layer, shard, give, ylen, 10 + j, me, 1 - grp).start()
        to_sibling(layer, shard, mine, zlen)

    def landed_y(layer, j, other):
        shard = level_of(j) * 2 + (1 - side if other else side)
        copy_to(layer, shard, lack, ylen, (10 if other else 7) + j, me, grp).wait_recv()
        to_sibling(layer, shard, lack, ylen)

    def do(layer, *events):
        for event in events:
            kind, j = event[0], int(event[1:] or 0)
            if kind == "s":
                send_own(layer)
            elif kind == "z":
                landed_z(layer, j)
            elif kind == "o":
                landed_own(layer)
            elif kind == "x":
                landed_x(layer, j)
            elif kind == "y":
                landed_y(layer, j, False)
            else:
                landed_y(layer, j, True)

    def sibling_done(layer):
        part = wbuf.at[
            layer,
            pl.ds(0, (count - 1) * rows),
            pl.ds(pl.multiple_of(sib * half, 128), half),
        ]
        remote(part, part, sib_send.at[layer], sib_recv.at[layer], me, sib).wait_recv()

    own_rows = pl.ds(pl.multiple_of(me * rows, 16), rows)
    stage[0].wait()
    stage[1].wait()
    for layer in range(layers):
        wbuf[layer, own_rows, : 3 * feat] = stage_q[layer]
        wbuf[layer, own_rows, 3 * feat :] = stage_o[layer]
    pl.semaphore_wait(barrier, 2 * count)
    do(0, "s")

    stage[2].wait()
    gap = -(-videos * patch_dev // 8) * 8
    r, c = iota((count * gap, 1), 0), iota((count * gap, tokens), 1)
    place = lax.rem(r, gap)
    source = jnp.where(place < videos * patch_dev, place * fr_dev + lax.div(r, gap), -1)
    pick = jnp.where(c == source, 1.0, 0.0).astype(jnp.bfloat16)
    moved = dot_f32(pick, stage_x[...].reshape(tokens, width), (1, 0))
    for k in range(count):
        xsend[k] = moved[k * gap : k * gap + videos * patch_dev].astype(jnp.bfloat16)
    for k in range(1, count):
        peer = lax.rem(me + k, count)
        remote(xsend.at[peer], xin.at[me], in_send, in_recv, peer, core).start()
    xin[me] = xsend[me]

    heads_map = jnp.where(
        (iota((heads, feat), 1) >= iota((heads, 1), 0) * head_size)
        & (iota((heads, feat), 1) < (iota((heads, 1), 0) + 1) * head_size),
        1.0,
        0.0,
    )
    spread = jnp.where(
        lax.rem(iota((head_size, feat), 1), head_size) == iota((head_size, feat), 0), 1.0, 0.0
    )
    gains = dot_exact(gain_ref[...].reshape(layers * 2, head_size), spread, (1, 0))
    params = [
        [tab_ref[i, layer : layer + 1] + mgain_ref[i, layer : layer + 1] * emb_ref[...] for i in range(3)]
        for layer in range(layers)
    ]

    def project(layer, mixed):
        joint = jnp.dot(mixed, wbuf[layer, :, : 3 * feat], preferred_element_type=jnp.float32)
        gain = gains[2 * layer : 2 * layer + 1], gains[2 * layer + 1 : 2 * layer + 2]
        query = norm_heads(joint[:, :feat], gain[0], heads_map, head_size)
        key = norm_heads(joint[:, feat : 2 * feat], gain[1], heads_map, head_size)
        return query, key, joint[:, 2 * feat :].astype(jnp.bfloat16)

    def update(layer, values, attended):
        added = dot_f32(attended, wbuf[layer, :, 3 * feat :], (1, 1))
        return values + params[layer][2] * added

    do(0, "z0", "o")
    remote(
        xsend.at[pl.ds(0, count - 1)], xin.at[pl.ds(0, count - 1)], in_send, in_recv, me, core
    ).wait_recv()
    size = videos * patch_dev
    for k in range(count):
        xf[k * size : (k + 1) * size, :] = xin[k].astype(jnp.float32)
    mixed = norm_tokens(xf[...], params[0])
    do(0, "z1", "x0", "y0", "z2")
    do(1, "s")
    do(0, "x1", "y1", "x2", "y2", "w0", "w1")
    do(1, "z0")
    do(0, "w2")
    sibling_done(0)
    query, key, value = project(0, mixed)
    part_of = lambda n: lax.rem(lax.div(iota((tokens, 1), 0), patch_dev), 2) if n else lax.rem(
        lax.div(iota((1, tokens), 1), patch_dev), 2
    )
    do(1, "o")
    plan = {1: ("z1",), 3: ("x0",), 5: ("y0",), 7: ("z2",)}
    attended = attend_heads(
        query, key, value, heads_map, part_of(1) == part_of(0), att, head_size,
        lambda head: do(1, *plan.get(head, ())),
    )
    xf[...] = update(0, xf[...], attended)

    frame = core * count + me
    for k in range(count):
        for video in range(videos):
            low = (k * videos + video) * patch_dev
            mid_send[video * count + k] = xf[low : low + patch_dev, :].astype(jnp.bfloat16)
    for s in range(2):
        for k in range(count):
            if k or s:
                peer, video = lax.rem(me + k, count), lax.rem(core + s, 2)
                remote(
                    mid_send.at[video * count + peer],
                    mid_recv.at[frame],
                    mid_ssem,
                    mid_rsem,
                    peer,
                    video,
                ).start()
    mid_recv[frame] = mid_send[frame]
    do(1, "x1", "y1", "x2", "y2", "w0", "w1", "w2")
    remote(
        mid_send.at[pl.ds(0, 2 * count - 1)],
        mid_recv.at[pl.ds(0, 2 * count - 1)],
        mid_ssem,
        mid_rsem,
        me,
        core,
    ).wait_recv()
    for k in range(2 * count):
        low = k * patch_dev
        xf[low : low + patch_dev, :] = mid_recv[k].astype(jnp.float32)
    mixed = norm_tokens(xf[...], params[1])
    sibling_done(1)
    query, key, value = project(1, mixed)
    same = lax.rem(iota((tokens, 1), 0), patch_dev) == lax.rem(iota((1, tokens), 1), patch_dev)
    attended = attend_heads(
        query, key, value, heads_map, same, att, head_size, lambda head: None
    )
    final = update(1, xf[...], attended).astype(jnp.bfloat16)
    r, c = iota((tokens, 1), 0), iota((tokens, tokens), 1)
    in_half = lax.rem(r, tokens // 2)
    source = (
        lax.div(r, tokens // 2) * fr_dev + lax.rem(in_half, fr_dev)
    ) * patch_dev + lax.div(in_half, fr_dev)
    pick = jnp.where(c == source, 1.0, 0.0).astype(jnp.bfloat16)
    res[...] = dot_f32(pick, final, (1, 0)).astype(jnp.bfloat16).reshape(res.shape)
    fin = remote(res.at[sib], out_ref.at[core], fin_send, fin_recv, me, sib)
    fin.start()
    out_ref[core] = res[core]
    for layer in range(layers):
        part = wbuf.at[
            layer,
            pl.ds(0, (count - 1) * rows),
            pl.ds(pl.multiple_of(core * half, 128), half),
        ]
        remote(part, part, ici_send.at[layer], sib_recv.at[layer], me, sib).wait_send()
        remote(part, part, sib_send.at[layer], sib_recv.at[layer], me, sib).wait_send()
    remote(
        xsend.at[pl.ds(0, count - 1)], xin.at[pl.ds(0, count - 1)], in_send, in_recv, me, core
    ).wait_send()
    remote(
        mid_send.at[pl.ds(0, 2 * count - 1)],
        mid_recv.at[pl.ds(0, 2 * count - 1)],
        mid_ssem,
        mid_rsem,
        me,
        core,
    ).wait_send()
    fin.wait_send()
    remote(out_ref.at[sib], out_ref.at[sib], fin_send, fin_recv, me, sib).wait_recv()


def fused_device(video_tokens, timestep, w_qkv, w_out, qk_gain, mod_table, mod_gain):
    videos, fr_dev, patch_dev, width = video_tokens.shape
    layers, rows, _ = w_qkv.shape
    head_size = qk_gain.shape[2]
    feat = w_out.shape[1]
    tokens = videos * fr_dev * patch_dev
    embed = time_embed(timestep, width)
    vmem = pl.BlockSpec(memory_space=pltpu.VMEM)
    hbm = pl.BlockSpec(memory_space=pl.ANY)
    count = fr_dev
    bf16, f32 = jnp.bfloat16, jnp.float32
    dma = pltpu.SemaphoreType.DMA
    out = pl.pallas_call(
        functools.partial(fused_kernel, head_size),
        out_shape=jax.ShapeDtypeStruct((videos, patch_dev, fr_dev, width), bf16),
        in_specs=[vmem] * 4 + [hbm] * 3,
        out_specs=vmem,
        scratch_shapes=[
            pltpu.VMEM((layers, count * rows, 4 * feat), bf16),
            pltpu.VMEM((layers, rows, 3 * feat), bf16),
            pltpu.VMEM((layers, rows, feat), bf16),
            pltpu.VMEM((videos, patch_dev, fr_dev, width), bf16),
            pltpu.VMEM((count, videos * patch_dev, width), bf16),
            pltpu.VMEM((count, videos * patch_dev, width), bf16),
            pltpu.VMEM((2 * count, patch_dev, width), bf16),
            pltpu.VMEM((2 * count, patch_dev, width), bf16),
            pltpu.VMEM((tokens, width), f32),
            pltpu.VMEM((tokens, feat), f32),
            pltpu.VMEM((2, patch_dev, fr_dev, width), bf16),
            dma((3,)),
            dma((layers,)),
            dma((layers, 13)),
            dma((layers,)),
            dma((layers,)),
            dma,
            dma,
            dma,
            dma,
            dma,
            dma,
        ],
        compiler_params=pltpu.CompilerParams(
            collective_id=0, has_side_effects=True, vmem_limit_bytes=56 * 1024 * 1024
        ),
        name="blocks",
    )(
        embed[None],
        qk_gain,
        mod_table.transpose(1, 0, 2),
        mod_gain.transpose(1, 0, 2),
        video_tokens.transpose(0, 2, 1, 3),
        w_qkv,
        w_out.transpose(0, 2, 1),
    )
    return out.transpose(0, 2, 1, 3)


def choose_device(video_tokens, timestep, w_qkv, *rest):
    videos, fr_dev, _, _ = video_tokens.shape
    fits = videos == 2 and fr_dev == 8 and w_qkv.shape[1] % 16 == 0
    run = fused_device if fits else per_device
    return run(video_tokens, timestep, w_qkv, *rest)


def solution(mesh):
    placed = (
        P("grp", "frame", "patch", None),
        P("grp"),
        P(None, "patch", None),
        P(None, None, "patch"),
        P(),
        P(),
        P(),
    )
    ring = (mesh.shape["grp"], mesh.shape["patch"], mesh.shape["frame"]) == (2, 8, 2)
    return jax.shard_map(
        choose_device if ring else per_device,
        mesh=mesh,
        in_specs=placed,
        out_specs=P("grp", "frame", "patch", None),
        check_vma=False,
    )
```

```python
import functools
import math

import jax
import jax.numpy as jnp
import numpy as np
from jax import lax
from jax.experimental import pallas as pl
from jax.experimental.pallas import tpu as pltpu
from jax.sharding import PartitionSpec as P


def time_embed(timestep, width):
    half_width = width // 2
    freqs = jnp.exp(-math.log(10000.0) * jnp.arange(half_width, dtype=jnp.float32) / half_width)
    angles = timestep[0].astype(jnp.float32) * freqs
    return jnp.concatenate([jnp.cos(angles), jnp.sin(angles)])


def modulate(tokens, table, gains, embed):
    params = table + gains * embed[None, :]
    values = tokens.astype(jnp.float32)
    centre = jnp.mean(values, axis=-1, keepdims=True)
    centred = values - centre
    spread = jnp.mean(centred * centred, axis=-1, keepdims=True)
    normed = centred * lax.rsqrt(spread + 1e-06)
    return ((normed * (1.0 + params[1]) + params[0]).astype(jnp.bfloat16), params[2])


def head_norm(values, gain):
    meansq = jnp.mean(values * values, axis=-1, keepdims=True)
    return (values * lax.rsqrt(meansq + 1e-06) * gain).astype(jnp.bfloat16)


def fetch_weights(qkv_rows, out_cols):
    return (
        lax.all_gather(qkv_rows, "patch", axis=0, tiled=True),
        lax.all_gather(out_cols, "patch", axis=1, tiled=True),
    )


def attend_items(stacked):
    head_size = stacked.shape[-1]
    query = stacked[0, 0]
    key = stacked[1, 0]
    value = stacked[2, 0]
    scores = jnp.einsum("nqd,nkd->nqk", query, key, preferred_element_type=jnp.float32) / math.sqrt(
        head_size
    )
    raised = jnp.exp(scores)
    total = jnp.sum(raised, axis=-1, keepdims=True)
    summed = jnp.einsum(
        "nqk,nkd->nqd", raised.astype(jnp.bfloat16), value, preferred_element_type=jnp.float32
    )
    return (summed / total).astype(jnp.bfloat16)[None]


def spatial(query, key, value, videos, fr_dev, patch_dev):
    rows, heads, head_size = query.shape
    groups = lax.axis_size("patch")
    per_group = videos * fr_dev * heads // groups
    stacked = jnp.stack([query, key, value])
    stacked = stacked.reshape(3, videos * fr_dev, patch_dev, heads, head_size)
    stacked = stacked.transpose(0, 1, 3, 2, 4).reshape(3, groups, per_group, patch_dev, head_size)
    attended = attend_items(
        lax.all_to_all(stacked, "patch", split_axis=1, concat_axis=3, tiled=True)
    )
    returned = lax.all_to_all(attended, "patch", split_axis=2, concat_axis=0, tiled=True)
    returned = returned.reshape(videos * fr_dev, heads, patch_dev, head_size).transpose(0, 2, 1, 3)
    return returned.reshape(rows, heads * head_size)


def frame_attend(query, key, value, heads):
    videos, q_frames, patches, feat = query.shape
    k_frames = key.shape[1]
    head_size = feat // heads
    query = query.reshape(videos, q_frames, patches, heads, head_size)
    key = key.reshape(videos, k_frames, patches, heads, head_size)
    value = value.reshape(videos, k_frames, patches, heads, head_size)
    scores = jnp.einsum(
        "bfphd,bgphd->bphfg", query, key, preferred_element_type=jnp.float32
    ) / math.sqrt(head_size)
    raised = jnp.exp(scores)
    total = jnp.sum(raised, axis=-1)
    summed = jnp.einsum(
        "bphfg,bgphd->bfphd", raised.astype(jnp.bfloat16), value, preferred_element_type=jnp.float32
    )
    result = summed / total.transpose(0, 3, 1, 2)[..., None]
    return result.astype(jnp.bfloat16).reshape(videos, q_frames, patches, feat)


def temporal(query, key, value, videos, fr_dev, patch_dev):
    rows, heads, head_size = query.shape
    feat = heads * head_size
    query4 = query.reshape(videos, fr_dev, patch_dev, feat)
    key4 = key.reshape(videos, fr_dev, patch_dev, feat)
    value4 = value.reshape(videos, fr_dev, patch_dev, feat)
    joined = jnp.concatenate([query4, key4, value4], axis=3)
    swapped = lax.all_to_all(joined, "frame", split_axis=2, concat_axis=1, tiled=True)
    result = frame_attend(
        swapped[..., :feat], swapped[..., feat : 2 * feat], swapped[..., 2 * feat :], heads
    )
    returned = lax.all_to_all(result, "frame", split_axis=1, concat_axis=2, tiled=True)
    return returned.reshape(rows, feat)


def per_device(video_tokens, timestep, w_qkv, w_out, qk_gain, mod_table, mod_gain):
    videos, fr_dev, patch_dev, width = video_tokens.shape
    rows = videos * fr_dev * patch_dev
    head_size = qk_gain.shape[2]
    heads = w_out.shape[1] // head_size
    embed = time_embed(timestep, width)
    tokens = video_tokens.reshape(rows, width)
    for layer in range(2):
        qkv_full, out_full = fetch_weights(w_qkv[layer], w_out[layer])
        mixed, gate = modulate(tokens, mod_table[layer], mod_gain[layer], embed)
        joint = jnp.dot(mixed, qkv_full, preferred_element_type=jnp.float32)
        joint = joint.reshape(rows, 3, heads, head_size)
        query = head_norm(joint[:, 0], qk_gain[layer, 0])
        key = head_norm(joint[:, 1], qk_gain[layer, 1])
        value = joint[:, 2].astype(jnp.bfloat16)
        if layer == 0:
            attended = spatial(query, key, value, videos, fr_dev, patch_dev)
        else:
            attended = temporal(query, key, value, videos, fr_dev, patch_dev)
        update = jnp.dot(attended, out_full, preferred_element_type=jnp.float32)
        tokens = (tokens.astype(jnp.float32) + gate * update).astype(jnp.bfloat16)
    return tokens.reshape(videos, fr_dev, patch_dev, width)


MESH = pl.DeviceIdType.MESH
HIGHEST = lax.Precision.HIGHEST


SPLIT = ()
PLAN = (
    ("0a", "0s",),
    ("0z00", "0x30", "1a", "0z01",),
    ("0x31", "1s", "0x00", "1z00", "0w30", "1x30", "0z10", "1z01", "0y0", "1x31", "0x01", "1x00", "0z11", "1w30", "0x10", "1z10", "0w00", "1y0", "0z20", "1x01", "0w01", "1z11", "0y1", "1x10", "0x11", "1w00", "0z21", "1z20", "0w10", "1w01", "0x20", "1y1", "0y2", "1x11", "0w11", "1z21", "0x21", "1w10", "0w20", "1x20",),
    ("1y2",),
    (),
    {1: ("1w11",), 3: ("1x21",), 5: ("1w20",)},
    (),
    (),
)


def time_row(timestep, width):
    half_width = width // 2
    column = lax.broadcasted_iota(jnp.int32, (1, width), 1)
    steps = lax.rem(column, half_width).astype(jnp.float32)
    angles = timestep[0].astype(jnp.float32) * jnp.exp(-math.log(10000.0) * steps / half_width)
    return jnp.where(column < half_width, jnp.cos(angles), jnp.sin(angles))


def dot_f32(a, b, contract):
    return lax.dot_general(
        a, b, ((contract[:1], contract[1:]), ((), ())), preferred_element_type=jnp.float32
    )


def dot_exact(a, b, contract):
    return lax.dot_general(
        a,
        b,
        ((contract[:1], contract[1:]), ((), ())),
        precision=HIGHEST,
        preferred_element_type=jnp.float32,
    )


def norm_tokens(values, params):
    centre = jnp.mean(values, axis=-1, keepdims=True)
    centred = values - centre
    spread = jnp.mean(centred * centred, axis=-1, keepdims=True)
    normed = centred * lax.rsqrt(spread + 1e-06)
    return (normed * (1.0 + params[1]) + params[0]).astype(jnp.bfloat16)


def two_parts(values):
    high = values.astype(jnp.bfloat16)
    return high, (values - high.astype(jnp.float32)).astype(jnp.bfloat16)


def norm_heads(values, gain, heads_map, head_size):
    high, low = two_parts(values * values)
    total = dot_f32(high, heads_map, (1, 1)) + dot_f32(low, heads_map, (1, 1))
    scale = jnp.concatenate(two_parts(lax.rsqrt(total / head_size + 1e-06)), axis=1)
    wide = dot_f32(scale, jnp.concatenate([heads_map] * 2, axis=0), (1, 0))
    return (values * wide * gain).astype(jnp.bfloat16)


def attend_heads(query, key, value, heads_map, mask, att_ref, head_size, between):
    feat = query.shape[1]
    att_ref[...] = jnp.zeros_like(att_ref)
    for head in range(feat // head_size):
        low = head * head_size // 128 * 128
        high = min(-(-(head + 1) * head_size // 128) * 128, feat)
        lanes = heads_map[head : head + 1, low:high]
        scores = dot_f32(query[:, low:high] * lanes, key[:, low:high], (1, 1))
        raised = jnp.where(mask, jnp.exp(scores * (1.0 / math.sqrt(head_size))), 0.0)
        total = jnp.sum(raised, axis=-1, keepdims=True)
        summed = dot_f32(raised.astype(jnp.bfloat16), value[:, low:high] * lanes, (1, 0))
        att_ref[:, low:high] += summed / total
        between(head)
    return att_ref[...].astype(jnp.bfloat16)


def iota(shape, dim):
    return lax.broadcasted_iota(jnp.int32, shape, dim)


def fused_kernel(
    head_size, emb_ref, gain_ref, tab_ref, mgain_ref, x_hbm, wq_hbm, wo_hbm, out_ref,
    wbuf, stage_q, stage_o, stage_x, xsend, xin, mid_send, mid_recv, xf, att, res,
    local_sem, ici_send, ici_recv, sib_send, sib_recv,
    in_send, in_recv, mid_ssem, mid_rsem, fin_send, fin_recv, z_send,
):
    videos, patch_dev, fr_dev, width = x_hbm.shape
    layers, rows, _ = wq_hbm.shape
    feat = wo_hbm.shape[2]
    heads = feat // head_size
    count = fr_dev
    tokens = videos * patch_dev * fr_dev
    half = wbuf.shape[2] // 2
    grp = lax.axis_index("grp")
    me = lax.axis_index("patch")
    core = lax.axis_index("frame")
    sib = 1 - core
    level, side = lax.div(me, 2), lax.rem(me, 2)
    across = level * 2 + 1 - side
    piece = rows // 3
    pair = videos * count
    whole = patch_dev // 8 * 8
    rest = patch_dev - whole
    per = 8 // rest
    packs = -(-width // (128 * per))

    stage = [
        pltpu.make_async_copy(wq_hbm, stage_q, local_sem.at[0]),
        pltpu.make_async_copy(wo_hbm, stage_o, local_sem.at[1]),
        pltpu.make_async_copy(x_hbm, stage_x, local_sem.at[2]),
    ]
    for copy in stage:
        copy.start()

    barrier = pltpu.get_barrier_semaphore()
    for k in range(count):
        for s in range(2):
            if k or s:
                pl.semaphore_signal(
                    barrier,
                    inc=1,
                    device_id=(grp, lax.rem(me + k, count), lax.rem(core + s, 2)),
                    device_id_type=MESH,
                )
    pl.semaphore_signal(
        barrier, inc=1, device_id=(1 - grp, me, core), device_id_type=MESH
    )

    def remote(src, dst, send_sem, recv_sem, patch, frame, to_grp=grp):
        return pltpu.make_async_remote_copy(
            src_ref=src,
            dst_ref=dst,
            send_sem=send_sem,
            recv_sem=recv_sem,
            device_id=(to_grp, patch, frame),
            device_id_type=MESH,
        )

    def block(layer, shard, start, size, of=core):
        first = pl.multiple_of(shard * rows + start, 16)
        return wbuf.at[
            layer, pl.ds(first, size), pl.ds(pl.multiple_of(of * half, 128), half)
        ]

    def to_sibling(layer, shard, start):
        part = block(layer, shard, start, piece)
        remote(part, part, sib_send.at[layer], sib_recv.at[layer], me, sib).start()

    upper = lax.div(level, 2)
    inner = lax.rem(level + upper, 2)

    def mirrored(i):
        return (1 - upper) * i + upper * (3 - i)

    def level_of(j):
        if j == 3:
            return level
        return mirrored(j + jnp.where(j < inner, 0, 1))

    def when(cond, act):
        pl.when(cond)(act)

    start_of = (grp * 2 * piece, piece)
    lacking = ((1 - grp) * 2 * piece, piece)

    def z_to(layer, source, target, q):
        part = block(layer, source * 2 + side, start_of[q], piece)
        return remote(
            part, part, z_send.at[layer], ici_recv.at[layer, q, source], target * 2 + side, core
        )

    def x_to(layer, source, shard, q, patch):
        part = block(layer, shard, start_of[q], piece)
        return remote(
            part, part, ici_send.at[layer], ici_recv.at[layer, 2 + q, source], patch, core
        )

    def y_to(layer, kind, source, shard, start, to_grp):
        part = block(layer, shard, start, piece)
        return remote(
            part, part, ici_send.at[layer], ici_recv.at[layer, kind, source], me, core, to_grp
        )

    def send_z(layer):
        for q in range(2):
            z_to(layer, level, mirrored(1 - inner), q).start()
            when(inner == 1, lambda q=q: z_to(layer, level, mirrored(2), q).start())

    def send_x(layer):
        for q in range(2):
            x_to(layer, level, me, q, across).start()

    def by_x(j):
        return grp == j if j in SPLIT else None

    def landed_z(layer, j, q):
        source = level_of(j)
        shard = source * 2 + side
        z_to(layer, source, level, q).wait_recv()
        when(
            inner == 1,
            lambda: z_to(layer, source, mirrored(2 if j == 0 else 0), q).start(),
        )
        if q == 0 or j not in SPLIT:
            x_to(layer, source, shard, q, across).start()
        else:
            when(by_x(j), lambda: x_to(layer, source, shard, q, across).start())
        if q == 0:
            y_to(layer, 4, source, shard, start_of[0], 1 - grp).start()
        to_sibling(layer, shard, start_of[q])

    def landed_x(layer, j, q):
        source = level_of(j)
        shard = source * 2 + 1 - side

        def take():
            x_to(layer, source, shard, q, me).wait_recv()
            if q == 0 or j in SPLIT:
                y_to(layer, 5 + q, source, shard, start_of[q], 1 - grp).start()
            to_sibling(layer, shard, start_of[q])

        if q == 0 or j not in SPLIT:
            take()
        else:
            when(by_x(j), take)

    def landed_y(layer, j):
        source = level_of(j)
        shard = source * 2 + side
        y_to(layer, 4, source, shard, lacking[0], grp).wait_recv()
        to_sibling(layer, shard, lacking[0])

    def landed_w(layer, j, q):
        source = level_of(j)
        shard = source * 2 + 1 - side

        def take():
            y_to(layer, 5 + q, source, shard, lacking[q], grp).wait_recv()
            to_sibling(layer, shard, lacking[q])

        if q == 0:
            take()
        elif j in SPLIT:
            when(grp != j, take)

    def do(events):
        for event in events:
            layer, kind = int(event[0]), event[1]
            args = [int(digit) for digit in event[2:]]
            {"a": send_z, "s": send_x, "z": landed_z, "x": landed_x, "y": landed_y, "w": landed_w}[
                kind
            ](layer, *args)

    def sibling_done(layer):
        part = wbuf.at[
            layer,
            pl.ds(0, (count - 1) * rows),
            pl.ds(pl.multiple_of(sib * half, 128), half),
        ]
        remote(part, part, sib_send.at[layer], sib_recv.at[layer], me, sib).wait_recv()

    own_rows = pl.ds(pl.multiple_of(me * rows, 16), rows)
    stage[0].wait()
    stage[1].wait()
    for layer in range(layers):
        wbuf[layer, own_rows, : 3 * feat] = stage_q[layer]
        wbuf[layer, own_rows, 3 * feat :] = stage_o[layer]
    pl.semaphore_wait(barrier, 2 * count)
    do(PLAN[0])

    stage[2].wait()
    size = videos * patch_dev
    gap = -(-size // 8) * 8
    r, c = iota((count * gap, 1), 0), iota((count * gap, tokens), 1)
    place, frame_of = lax.rem(r, gap), lax.div(r, gap)
    after = place - videos * whole
    first = lax.div(place, whole) * patch_dev + lax.rem(place, whole)
    last = lax.div(after, rest) * patch_dev + whole + lax.rem(after, rest)
    source = jnp.where(after < 0, first, last) * fr_dev + frame_of
    pick = jnp.where((c == source) & (place < size), 1.0, 0.0).astype(jnp.bfloat16)
    moved = dot_f32(pick, stage_x[...].reshape(tokens, width), (1, 0))
    for k in range(count):
        xsend[k] = moved[k * gap : k * gap + size].astype(jnp.bfloat16)
    for k in range(1, count):
        peer = lax.rem(me + k, count)
        remote(xsend.at[peer], xin.at[me], in_send, in_recv, peer, core).start()
    xin[me] = xsend[me]

    heads_map = jnp.where(
        (iota((heads, feat), 1) >= iota((heads, 1), 0) * head_size)
        & (iota((heads, feat), 1) < (iota((heads, 1), 0) + 1) * head_size),
        1.0,
        0.0,
    ).astype(jnp.bfloat16)
    spread = jnp.where(
        lax.rem(iota((head_size, feat), 1), head_size) == iota((head_size, feat), 0), 1.0, 0.0
    )
    gains = dot_exact(gain_ref[...].reshape(layers * 2, head_size), spread, (1, 0))
    params = [
        [tab_ref[i, layer : layer + 1] + mgain_ref[i, layer : layer + 1] * emb_ref[...] for i in range(3)]
        for layer in range(layers)
    ]

    def project(layer, mixed):
        joint = jnp.dot(mixed, wbuf[layer, :, : 3 * feat], preferred_element_type=jnp.float32)
        gain = gains[2 * layer : 2 * layer + 1], gains[2 * layer + 1 : 2 * layer + 2]
        query = norm_heads(joint[:, :feat], gain[0], heads_map, head_size)
        key = norm_heads(joint[:, feat : 2 * feat], gain[1], heads_map, head_size)
        return query, key, joint[:, 2 * feat :].astype(jnp.bfloat16)

    def update(layer, values, attended):
        added = dot_f32(attended, wbuf[layer, :, 3 * feat :], (1, 1))
        return values + params[layer][2] * added

    def item(r, main, left):
        return jnp.where(r < whole * pair, main(r), left(r - whole * pair))

    def rows_and_columns(main, left):
        return item(iota((tokens, 1), 0), main, left), item(iota((1, tokens), 1), main, left)

    fold = per * pair * rest
    r, c = iota((pair * 8, 1), 0), iota((pair * 8, fold), 1)
    part, within = lax.div(lax.rem(r, 8), rest), lax.rem(lax.rem(r, 8), rest)
    source = part * pair * rest + lax.div(r, 8) * rest + within
    folding = jnp.where(c == source, 1.0, 0.0).astype(jnp.bfloat16)

    do(PLAN[1])
    remote(
        xsend.at[pl.ds(0, count - 1)], xin.at[pl.ds(0, count - 1)], in_send, in_recv, me, core
    ).wait_recv()
    for k in range(count):
        got = xin[k].astype(jnp.float32)
        low, step = k * videos * whole, videos * rest
        xf[low : low + videos * whole, :] = got[: videos * whole]
        low = pair * whole + k * step
        xf[low : low + step, :] = got[videos * whole :]
    mixed = norm_tokens(xf[...], params[0])
    do(PLAN[2])
    sibling_done(0)
    do(PLAN[3])
    query, key, value = project(0, mixed)
    do(PLAN[4])
    down, along = rows_and_columns(
        lambda n: lax.rem(lax.div(n, whole), videos), lambda n: lax.rem(lax.div(n, rest), videos)
    )
    attended = attend_heads(
        query, key, value, heads_map, down == along, att, head_size,
        lambda head: do(PLAN[5].get(head, ())),
    )
    done = update(0, xf[...], attended).astype(jnp.bfloat16)

    frame = core * count + me
    left = done[whole * pair :]
    lanes = [left[:, low : low + 128] for low in range(0, width, 128)]
    lanes += [jnp.zeros_like(lanes[0])] * (packs * per - len(lanes))
    packed = [
        dot_f32(folding, jnp.concatenate(lanes[n * per : (n + 1) * per], axis=0), (1, 0))
        for n in range(packs)
    ]
    full = done[: whole * pair].astype(jnp.float32)
    for k in range(pair):
        rows_k = slice(k * whole, (k + 1) * whole)
        mid_send[k, :, :width] = full[rows_k].astype(jnp.bfloat16)
        for n in range(packs):
            low = width + n * 128
            mid_send[k, :, low : low + 128] = packed[n][k * 8 : k * 8 + 8].astype(jnp.bfloat16)
    for s in range(2):
        for k in range(count):
            if k or s:
                peer, video = lax.rem(me + k, count), lax.rem(core + s, 2)
                remote(
                    mid_send.at[peer * videos + video],
                    mid_recv.at[frame],
                    mid_ssem,
                    mid_rsem,
                    peer,
                    video,
                ).start()
    mid_recv[frame] = mid_send[me * videos + core]
    do(PLAN[6])
    remote(
        mid_send.at[pl.ds(0, pair - 1)],
        mid_recv.at[pl.ds(0, pair - 1)],
        mid_ssem,
        mid_rsem,
        me,
        core,
    ).wait_recv()
    got = [mid_recv[k].astype(jnp.float32) for k in range(pair)]
    for k in range(pair):
        xf[k * whole : (k + 1) * whole, :] = got[k][:, :width]
    for n in range(packs):
        low = width + n * 128
        pack = jnp.concatenate([got[k][:, low : low + 128] for k in range(pair)], axis=0)
        spread_out = dot_f32(folding, pack.astype(jnp.bfloat16), (0, 0))
        for m in range(min(per, width // 128 - n * per)):
            lane = (n * per + m) * 128
            xf[whole * pair :, lane : lane + 128] = spread_out[
                m * pair * rest : (m + 1) * pair * rest
            ]
    mixed = norm_tokens(xf[...], params[1])
    do(PLAN[7])
    sibling_done(1)
    query, key, value = project(1, mixed)
    down, along = rows_and_columns(
        lambda n: lax.rem(n, whole), lambda n: whole + lax.rem(n, rest)
    )
    attended = attend_heads(
        query, key, value, heads_map, down == along, att, head_size, lambda head: None
    )
    final = update(1, xf[...], attended).astype(jnp.bfloat16)
    r, c = iota((tokens, 1), 0), iota((tokens, tokens), 1)
    in_half = lax.rem(r, tokens // 2)
    when_ = lax.div(r, tokens // 2) * fr_dev + lax.rem(in_half, fr_dev)
    where_ = lax.div(in_half, fr_dev)
    source = jnp.where(
        where_ < whole,
        when_ * whole + where_,
        whole * pair + when_ * rest + where_ - whole,
    )
    pick = jnp.where(c == source, 1.0, 0.0).astype(jnp.bfloat16)
    res[...] = dot_f32(pick, final, (1, 0)).astype(jnp.bfloat16).reshape(res.shape)
    fin = remote(res.at[sib], out_ref.at[core], fin_send, fin_recv, me, sib)
    fin.start()
    out_ref[core] = res[core]
    def span(layer, pieces):
        return wbuf.at[
            layer,
            pl.ds(0, pieces * piece),
            pl.ds(pl.multiple_of(core * half, 128), half),
        ]

    def drain(layer, pieces, sem):
        part = span(layer, pieces)
        remote(part, part, sem.at[layer], sib_recv.at[layer], me, sib).wait_send()

    for layer in range(layers):
        drain(layer, 15, ici_send)
        drain(layer, 3 * (count - 1), sib_send)
        when(inner == 1, lambda layer=layer: drain(layer, 10, z_send))
        when(inner == 0, lambda layer=layer: drain(layer, 2, z_send))
    remote(
        xsend.at[pl.ds(0, count - 1)], xin.at[pl.ds(0, count - 1)], in_send, in_recv, me, core
    ).wait_send()
    remote(
        mid_send.at[pl.ds(0, pair - 1)],
        mid_recv.at[pl.ds(0, pair - 1)],
        mid_ssem,
        mid_rsem,
        me,
        core,
    ).wait_send()
    fin.wait_send()
    remote(out_ref.at[sib], out_ref.at[sib], fin_send, fin_recv, me, sib).wait_recv()


def fused_device(video_tokens, timestep, w_qkv, w_out, qk_gain, mod_table, mod_gain):
    videos, fr_dev, patch_dev, width = video_tokens.shape
    layers, rows, _ = w_qkv.shape
    head_size = qk_gain.shape[2]
    feat = w_out.shape[1]
    tokens = videos * fr_dev * patch_dev
    embed = time_row(timestep, width)
    vmem = pl.BlockSpec(memory_space=pltpu.VMEM)
    hbm = pl.BlockSpec(memory_space=pl.ANY)
    count = fr_dev
    packed = width + -(-width // (1024 // (patch_dev % 8))) * 128
    bf16, f32 = jnp.bfloat16, jnp.float32
    dma = pltpu.SemaphoreType.DMA
    out = pl.pallas_call(
        functools.partial(fused_kernel, head_size),
        out_shape=jax.ShapeDtypeStruct((videos, patch_dev, fr_dev, width), bf16),
        in_specs=[vmem] * 4 + [hbm] * 3,
        out_specs=vmem,
        scratch_shapes=[
            pltpu.VMEM((layers, count * rows, 4 * feat), bf16),
            pltpu.VMEM((layers, rows, 3 * feat), bf16),
            pltpu.VMEM((layers, rows, feat), bf16),
            pltpu.VMEM((videos, patch_dev, fr_dev, width), bf16),
            pltpu.VMEM((count, videos * patch_dev, width), bf16),
            pltpu.VMEM((count, videos * patch_dev, width), bf16),
            pltpu.VMEM((2 * count, 8, packed), bf16),
            pltpu.VMEM((2 * count, 8, packed), bf16),
            pltpu.VMEM((tokens, width), f32),
            pltpu.VMEM((tokens, feat), f32),
            pltpu.VMEM((2, patch_dev, fr_dev, width), bf16),
            dma((3,)),
            dma((layers,)),
            dma((layers, 7, 4)),
            dma((layers,)),
            dma((layers,)),
            dma,
            dma,
            dma,
            dma,
            dma,
            dma,
            dma((layers,)),
        ],
        compiler_params=pltpu.CompilerParams(
            collective_id=0, has_side_effects=True, vmem_limit_bytes=56 * 1024 * 1024
        ),
        name="blocks",
    )(
        embed,
        qk_gain,
        mod_table.transpose(1, 0, 2),
        mod_gain.transpose(1, 0, 2),
        video_tokens.transpose(0, 2, 1, 3),
        w_qkv,
        w_out.transpose(0, 2, 1),
    )
    return out.transpose(0, 2, 1, 3)


def choose_device(video_tokens, timestep, w_qkv, *rest):
    videos, fr_dev, _, _ = video_tokens.shape
    fits = (videos, fr_dev) == (2, 8) and video_tokens.shape[2:] == (10, 1152) and w_qkv.shape[1] == 144
    run = fused_device if fits else per_device
    return run(video_tokens, timestep, w_qkv, *rest)


def solution(mesh):
    placed = (
        P("grp", "frame", "patch", None),
        P("grp"),
        P(None, "patch", None),
        P(None, None, "patch"),
        P(),
        P(),
        P(),
    )
    ring = (mesh.shape["grp"], mesh.shape["patch"], mesh.shape["frame"]) == (2, 8, 2)
    return jax.shard_map(
        choose_device if ring else per_device,
        mesh=mesh,
        in_specs=placed,
        out_specs=P("grp", "frame", "patch", None),
        check_vma=False,
    )
```

```python
import functools
import math

import jax
import jax.numpy as jnp
import numpy as np
from jax import lax
from jax.experimental import pallas as pl
from jax.experimental.pallas import tpu as pltpu
from jax.sharding import PartitionSpec as P


def time_embed(timestep, width):
    half_width = width // 2
    freqs = jnp.exp(-math.log(10000.0) * jnp.arange(half_width, dtype=jnp.float32) / half_width)
    angles = timestep[0].astype(jnp.float32) * freqs
    return jnp.concatenate([jnp.cos(angles), jnp.sin(angles)])


def modulate(tokens, table, gains, embed):
    params = table + gains * embed[None, :]
    values = tokens.astype(jnp.float32)
    centre = jnp.mean(values, axis=-1, keepdims=True)
    centred = values - centre
    spread = jnp.mean(centred * centred, axis=-1, keepdims=True)
    normed = centred * lax.rsqrt(spread + 1e-06)
    return ((normed * (1.0 + params[1]) + params[0]).astype(jnp.bfloat16), params[2])


def head_norm(values, gain):
    meansq = jnp.mean(values * values, axis=-1, keepdims=True)
    return (values * lax.rsqrt(meansq + 1e-06) * gain).astype(jnp.bfloat16)


def fetch_weights(qkv_rows, out_cols):
    return (
        lax.all_gather(qkv_rows, "patch", axis=0, tiled=True),
        lax.all_gather(out_cols, "patch", axis=1, tiled=True),
    )


def attend_items(stacked):
    head_size = stacked.shape[-1]
    query = stacked[0, 0]
    key = stacked[1, 0]
    value = stacked[2, 0]
    scores = jnp.einsum("nqd,nkd->nqk", query, key, preferred_element_type=jnp.float32) / math.sqrt(
        head_size
    )
    raised = jnp.exp(scores)
    total = jnp.sum(raised, axis=-1, keepdims=True)
    summed = jnp.einsum(
        "nqk,nkd->nqd", raised.astype(jnp.bfloat16), value, preferred_element_type=jnp.float32
    )
    return (summed / total).astype(jnp.bfloat16)[None]


def spatial(query, key, value, videos, fr_dev, patch_dev):
    rows, heads, head_size = query.shape
    groups = lax.axis_size("patch")
    per_group = videos * fr_dev * heads // groups
    stacked = jnp.stack([query, key, value])
    stacked = stacked.reshape(3, videos * fr_dev, patch_dev, heads, head_size)
    stacked = stacked.transpose(0, 1, 3, 2, 4).reshape(3, groups, per_group, patch_dev, head_size)
    attended = attend_items(
        lax.all_to_all(stacked, "patch", split_axis=1, concat_axis=3, tiled=True)
    )
    returned = lax.all_to_all(attended, "patch", split_axis=2, concat_axis=0, tiled=True)
    returned = returned.reshape(videos * fr_dev, heads, patch_dev, head_size).transpose(0, 2, 1, 3)
    return returned.reshape(rows, heads * head_size)


def frame_attend(query, key, value, heads):
    videos, q_frames, patches, feat = query.shape
    k_frames = key.shape[1]
    head_size = feat // heads
    query = query.reshape(videos, q_frames, patches, heads, head_size)
    key = key.reshape(videos, k_frames, patches, heads, head_size)
    value = value.reshape(videos, k_frames, patches, heads, head_size)
    scores = jnp.einsum(
        "bfphd,bgphd->bphfg", query, key, preferred_element_type=jnp.float32
    ) / math.sqrt(head_size)
    raised = jnp.exp(scores)
    total = jnp.sum(raised, axis=-1)
    summed = jnp.einsum(
        "bphfg,bgphd->bfphd", raised.astype(jnp.bfloat16), value, preferred_element_type=jnp.float32
    )
    result = summed / total.transpose(0, 3, 1, 2)[..., None]
    return result.astype(jnp.bfloat16).reshape(videos, q_frames, patches, feat)


def temporal(query, key, value, videos, fr_dev, patch_dev):
    rows, heads, head_size = query.shape
    feat = heads * head_size
    query4 = query.reshape(videos, fr_dev, patch_dev, feat)
    key4 = key.reshape(videos, fr_dev, patch_dev, feat)
    value4 = value.reshape(videos, fr_dev, patch_dev, feat)
    joined = jnp.concatenate([query4, key4, value4], axis=3)
    swapped = lax.all_to_all(joined, "frame", split_axis=2, concat_axis=1, tiled=True)
    result = frame_attend(
        swapped[..., :feat], swapped[..., feat : 2 * feat], swapped[..., 2 * feat :], heads
    )
    returned = lax.all_to_all(result, "frame", split_axis=1, concat_axis=2, tiled=True)
    return returned.reshape(rows, feat)


def per_device(video_tokens, timestep, w_qkv, w_out, qk_gain, mod_table, mod_gain):
    videos, fr_dev, patch_dev, width = video_tokens.shape
    rows = videos * fr_dev * patch_dev
    head_size = qk_gain.shape[2]
    heads = w_out.shape[1] // head_size
    embed = time_embed(timestep, width)
    tokens = video_tokens.reshape(rows, width)
    for layer in range(2):
        qkv_full, out_full = fetch_weights(w_qkv[layer], w_out[layer])
        mixed, gate = modulate(tokens, mod_table[layer], mod_gain[layer], embed)
        joint = jnp.dot(mixed, qkv_full, preferred_element_type=jnp.float32)
        joint = joint.reshape(rows, 3, heads, head_size)
        query = head_norm(joint[:, 0], qk_gain[layer, 0])
        key = head_norm(joint[:, 1], qk_gain[layer, 1])
        value = joint[:, 2].astype(jnp.bfloat16)
        if layer == 0:
            attended = spatial(query, key, value, videos, fr_dev, patch_dev)
        else:
            attended = temporal(query, key, value, videos, fr_dev, patch_dev)
        update = jnp.dot(attended, out_full, preferred_element_type=jnp.float32)
        tokens = (tokens.astype(jnp.float32) + gate * update).astype(jnp.bfloat16)
    return tokens.reshape(videos, fr_dev, patch_dev, width)


MESH = pl.DeviceIdType.MESH
HIGHEST = lax.Precision.HIGHEST


PLAN = (
    ("0a", "0s",),
    ("0z00", "1s", "0z10", "0f00", "0z01", "0f10", "0z11", "0z20", "0f20",),
    ("0x30", "1a", "1x30", "0y2", "0x00", "0f11", "0f01", "0x31", "0x10", "0z21", "1z00", "0f21", "0x20", "1z10", "0w30", "1f00", "0y0", "0w10", "1z11", "1z01", "0x11", "1f10", "0y1",),
    ("1w30", "0w00", "1z20", "0x21", "1f11", "0w20", "1f20", "0x01", "1f01", "1z21",),
    ("1x10",),
    {1: ("1f21",)},
    ("1x00", "1x31", "1w10", "1x11", "1y2", "1y0", "1y1", "1x20", "1w00", "1x21", "1x01", "1w20",),
    (),
)


def time_row(timestep, width):
    half_width = width // 2
    column = lax.broadcasted_iota(jnp.int32, (1, width), 1)
    steps = lax.rem(column, half_width).astype(jnp.float32)
    angles = timestep[0].astype(jnp.float32) * jnp.exp(-math.log(10000.0) * steps / half_width)
    return jnp.where(column < half_width, jnp.cos(angles), jnp.sin(angles))


def dot_f32(a, b, contract):
    return lax.dot_general(
        a, b, ((contract[:1], contract[1:]), ((), ())), preferred_element_type=jnp.float32
    )


def dot_exact(a, b, contract):
    return lax.dot_general(
        a,
        b,
        ((contract[:1], contract[1:]), ((), ())),
        precision=HIGHEST,
        preferred_element_type=jnp.float32,
    )


def norm_tokens(values, params):
    centre = jnp.mean(values, axis=-1, keepdims=True)
    centred = values - centre
    spread = jnp.mean(centred * centred, axis=-1, keepdims=True)
    normed = centred * lax.rsqrt(spread + 1e-06)
    return (normed * (1.0 + params[1]) + params[0]).astype(jnp.bfloat16)


def two_parts(values):
    high = values.astype(jnp.bfloat16)
    return high, (values - high.astype(jnp.float32)).astype(jnp.bfloat16)


def norm_heads(values, gain, heads_map, head_size):
    high, low = two_parts(values * values)
    total = dot_f32(high, heads_map, (1, 1)) + dot_f32(low, heads_map, (1, 1))
    scale = jnp.concatenate(two_parts(lax.rsqrt(total / head_size + 1e-06)), axis=1)
    wide = dot_f32(scale, jnp.concatenate([heads_map] * 2, axis=0), (1, 0))
    return (values * wide * gain).astype(jnp.bfloat16)


def attend_heads(query, key, value, heads_map, mask, att_ref, head_size, between):
    feat = query.shape[1]
    att_ref[...] = jnp.zeros_like(att_ref)
    for head in range(feat // head_size):
        low = head * head_size // 128 * 128
        high = min(-(-(head + 1) * head_size // 128) * 128, feat)
        lanes = heads_map[head : head + 1, low:high]
        scores = dot_f32(query[:, low:high] * lanes, key[:, low:high], (1, 1))
        raised = jnp.where(mask, jnp.exp(scores * (1.0 / math.sqrt(head_size))), 0.0)
        total = jnp.sum(raised, axis=-1, keepdims=True)
        summed = dot_f32(raised.astype(jnp.bfloat16), value[:, low:high] * lanes, (1, 0))
        att_ref[:, low:high] += summed / total
        between(head)
    return att_ref[...].astype(jnp.bfloat16)


def iota(shape, dim):
    return lax.broadcasted_iota(jnp.int32, shape, dim)


def fused_kernel(
    head_size, emb_ref, gain_ref, tab_ref, mgain_ref, x_hbm, wq_hbm, wo_hbm, out_ref,
    wbuf, stage_q, stage_o, stage_x, xsend, xin, mid_send, mid_recv, xf, att, res,
    local_sem, ici_send, ici_recv, sib_send, sib_recv,
    in_send, in_recv, mid_ssem, mid_rsem, fin_send, fin_recv, z_send,
):
    videos, patch_dev, fr_dev, width = x_hbm.shape
    layers, rows, _ = wq_hbm.shape
    feat = wo_hbm.shape[2]
    heads = feat // head_size
    count = fr_dev
    tokens = videos * patch_dev * fr_dev
    half = wbuf.shape[2] // 2
    grp = lax.axis_index("grp")
    me = lax.axis_index("patch")
    core = lax.axis_index("frame")
    sib = 1 - core
    level, side = lax.div(me, 2), lax.rem(me, 2)
    across = level * 2 + 1 - side
    piece = rows // 3
    pair = videos * count
    whole = patch_dev // 8 * 8
    rest = patch_dev - whole
    per = 8 // rest
    packs = -(-width // (128 * per))

    stage = [
        pltpu.make_async_copy(wq_hbm, stage_q, local_sem.at[0]),
        pltpu.make_async_copy(wo_hbm, stage_o, local_sem.at[1]),
        pltpu.make_async_copy(x_hbm, stage_x, local_sem.at[2]),
    ]
    for copy in stage:
        copy.start()

    barrier = pltpu.get_barrier_semaphore()
    for k in range(count):
        for s in range(2):
            if k or s:
                pl.semaphore_signal(
                    barrier,
                    inc=1,
                    device_id=(grp, lax.rem(me + k, count), lax.rem(core + s, 2)),
                    device_id_type=MESH,
                )
    pl.semaphore_signal(
        barrier, inc=1, device_id=(1 - grp, me, core), device_id_type=MESH
    )

    def remote(src, dst, send_sem, recv_sem, patch, frame, to_grp=grp):
        return pltpu.make_async_remote_copy(
            src_ref=src,
            dst_ref=dst,
            send_sem=send_sem,
            recv_sem=recv_sem,
            device_id=(to_grp, patch, frame),
            device_id_type=MESH,
        )

    def block(layer, shard, start, size, of=core):
        first = pl.multiple_of(shard * rows + start, 16)
        return wbuf.at[
            layer, pl.ds(first, size), pl.ds(pl.multiple_of(of * half, 128), half)
        ]

    def to_sibling(layer, shard, start):
        part = block(layer, shard, start, piece)
        remote(part, part, sib_send.at[layer], sib_recv.at[layer], me, sib).start()

    upper = lax.div(level, 2)
    inner = lax.rem(level + upper, 2)

    def mirrored(i):
        return (1 - upper) * i + upper * (3 - i)

    def level_of(j):
        if j == 3:
            return level
        return mirrored(j + jnp.where(j < inner, 0, 1))

    def when(cond, act):
        pl.when(cond)(act)

    start_of = (grp * 2 * piece, piece)
    lacking = ((1 - grp) * 2 * piece, piece)

    def z_to(layer, source, target, q):
        part = block(layer, source * 2 + side, start_of[q], piece)
        return remote(
            part, part, z_send.at[layer], ici_recv.at[layer, q, source], target * 2 + side, core
        )

    def x_to(layer, source, shard, q, patch):
        part = block(layer, shard, start_of[q], piece)
        return remote(
            part, part, ici_send.at[layer], ici_recv.at[layer, 2 + q, source], patch, core
        )

    def y_to(layer, kind, source, shard, start, to_grp):
        part = block(layer, shard, start, piece)
        return remote(
            part, part, ici_send.at[layer], ici_recv.at[layer, kind, source], me, core, to_grp
        )

    def send_z(layer):
        for q in range(2):
            z_to(layer, level, mirrored(1 - inner), q).start()
            when(inner == 1, lambda q=q: z_to(layer, level, mirrored(2), q).start())

    def send_x(layer):
        for q in range(2):
            x_to(layer, level, me, q, across).start()

    def pass_on(layer, j, q):
        source = level_of(j)
        shard = source * 2 + side
        x_to(layer, source, shard, q, across).start()
        if q == 0:
            y_to(layer, 4, source, shard, start_of[0], 1 - grp).start()

    def landed_z(layer, j, q):
        source = level_of(j)
        shard = source * 2 + side
        z_to(layer, source, level, q).wait_recv()
        when(
            inner == 1,
            lambda: z_to(layer, source, mirrored(2 if j == 0 else 0), q).start(),
        )
        to_sibling(layer, shard, start_of[q])

    def landed_x(layer, j, q):
        source = level_of(j)
        shard = source * 2 + 1 - side

        x_to(layer, source, shard, q, me).wait_recv()
        if q == 0:
            y_to(layer, 5, source, shard, start_of[0], 1 - grp).start()
        to_sibling(layer, shard, start_of[q])

    def landed_y(layer, j):
        source = level_of(j)
        shard = source * 2 + side
        y_to(layer, 4, source, shard, lacking[0], grp).wait_recv()
        to_sibling(layer, shard, lacking[0])

    def landed_w(layer, j, _):
        source = level_of(j)
        shard = source * 2 + 1 - side
        y_to(layer, 5, source, shard, lacking[0], grp).wait_recv()
        to_sibling(layer, shard, lacking[0])

    def do(events):
        for event in events:
            layer, kind = int(event[0]), event[1]
            args = [int(digit) for digit in event[2:]]
            actions[kind](layer, *args)

    actions = {
        "a": send_z,
        "s": send_x,
        "z": landed_z,
        "f": pass_on,
        "x": landed_x,
        "y": landed_y,
        "w": landed_w,
    }

    def sibling_done(layer):
        part = wbuf.at[
            layer,
            pl.ds(0, (count - 1) * rows),
            pl.ds(pl.multiple_of(sib * half, 128), half),
        ]
        remote(part, part, sib_send.at[layer], sib_recv.at[layer], me, sib).wait_recv()

    own_rows = pl.ds(pl.multiple_of(me * rows, 16), rows)
    stage[0].wait()
    stage[1].wait()
    for layer in range(layers):
        wbuf[layer, own_rows, : 3 * feat] = stage_q[layer]
        wbuf[layer, own_rows, 3 * feat :] = stage_o[layer]
    pl.semaphore_wait(barrier, 2 * count)
    do(PLAN[0])

    stage[2].wait()
    size = videos * patch_dev
    gap = -(-size // 8) * 8
    r, c = iota((count * gap, 1), 0), iota((count * gap, tokens), 1)
    place, frame_of = lax.rem(r, gap), lax.div(r, gap)
    after = place - videos * whole
    first = lax.div(place, whole) * patch_dev + lax.rem(place, whole)
    last = lax.div(after, rest) * patch_dev + whole + lax.rem(after, rest)
    source = jnp.where(after < 0, first, last) * fr_dev + frame_of
    pick = jnp.where((c == source) & (place < size), 1.0, 0.0).astype(jnp.bfloat16)
    moved = dot_f32(pick, stage_x[...].reshape(tokens, width), (1, 0))
    for k in range(count):
        xsend[k] = moved[k * gap : k * gap + size].astype(jnp.bfloat16)
    xin[me] = xsend[me]

    heads_map = jnp.where(
        (iota((heads, feat), 1) >= iota((heads, 1), 0) * head_size)
        & (iota((heads, feat), 1) < (iota((heads, 1), 0) + 1) * head_size),
        1.0,
        0.0,
    ).astype(jnp.bfloat16)
    spread = jnp.where(
        lax.rem(iota((head_size, feat), 1), head_size) == iota((head_size, feat), 0), 1.0, 0.0
    )
    gains = dot_exact(gain_ref[...].reshape(layers * 2, head_size), spread, (1, 0))
    params = [
        [tab_ref[i, layer : layer + 1] + mgain_ref[i, layer : layer + 1] * emb_ref[...] for i in range(3)]
        for layer in range(layers)
    ]

    def project(layer, mixed):
        joint = jnp.dot(mixed, wbuf[layer, :, : 3 * feat], preferred_element_type=jnp.float32)
        gain = gains[2 * layer : 2 * layer + 1], gains[2 * layer + 1 : 2 * layer + 2]
        query = norm_heads(joint[:, :feat], gain[0], heads_map, head_size)
        key = norm_heads(joint[:, feat : 2 * feat], gain[1], heads_map, head_size)
        return query, key, joint[:, 2 * feat :].astype(jnp.bfloat16)

    def update(layer, values, attended):
        added = dot_f32(attended, wbuf[layer, :, 3 * feat :], (1, 1))
        return values + params[layer][2] * added

    def item(r, main, left):
        return jnp.where(r < whole * pair, main(r), left(r - whole * pair))

    def rows_and_columns(main, left):
        return item(iota((tokens, 1), 0), main, left), item(iota((1, tokens), 1), main, left)

    fold = per * pair * rest
    r, c = iota((pair * 8, 1), 0), iota((pair * 8, fold), 1)
    part, within = lax.div(lax.rem(r, 8), rest), lax.rem(lax.rem(r, 8), rest)
    source = part * pair * rest + lax.div(r, 8) * rest + within
    folding = jnp.where(c == source, 1.0, 0.0).astype(jnp.bfloat16)

    do(PLAN[1])
    for k in range(1, count):
        peer = lax.rem(me + k, count)
        remote(xsend.at[peer], xin.at[me], in_send, in_recv, peer, core).start()
    do(PLAN[2])
    remote(
        xsend.at[pl.ds(0, count - 1)], xin.at[pl.ds(0, count - 1)], in_send, in_recv, me, core
    ).wait_recv()
    for k in range(count):
        got = xin[k].astype(jnp.float32)
        low, step = k * videos * whole, videos * rest
        xf[low : low + videos * whole, :] = got[: videos * whole]
        low = pair * whole + k * step
        xf[low : low + step, :] = got[videos * whole :]
    mixed = norm_tokens(xf[...], params[0])
    do(PLAN[3])
    sibling_done(0)
    do(PLAN[4])
    query, key, value = project(0, mixed)
    down, along = rows_and_columns(
        lambda n: lax.rem(lax.div(n, whole), videos), lambda n: lax.rem(lax.div(n, rest), videos)
    )
    attended = attend_heads(
        query, key, value, heads_map, down == along, att, head_size,
        lambda head: do(PLAN[5].get(head, ())),
    )
    done = update(0, xf[...], attended).astype(jnp.bfloat16)

    frame = core * count + me
    left = done[whole * pair :]
    lanes = [left[:, low : low + 128] for low in range(0, width, 128)]
    lanes += [jnp.zeros_like(lanes[0])] * (packs * per - len(lanes))
    packed = [
        dot_f32(folding, jnp.concatenate(lanes[n * per : (n + 1) * per], axis=0), (1, 0))
        for n in range(packs)
    ]
    full = done[: whole * pair].astype(jnp.float32)
    for k in range(pair):
        rows_k = slice(k * whole, (k + 1) * whole)
        mid_send[k, :, :width] = full[rows_k].astype(jnp.bfloat16)
        for n in range(packs):
            low = width + n * 128
            mid_send[k, :, low : low + 128] = packed[n][k * 8 : k * 8 + 8].astype(jnp.bfloat16)
    for s in range(2):
        for k in range(count):
            if k or s:
                peer, video = lax.rem(me + k, count), lax.rem(core + s, 2)
                remote(
                    mid_send.at[peer * videos + video],
                    mid_recv.at[frame],
                    mid_ssem,
                    mid_rsem,
                    peer,
                    video,
                ).start()
    mid_recv[frame] = mid_send[me * videos + core]
    do(PLAN[6])
    remote(
        mid_send.at[pl.ds(0, pair - 1)],
        mid_recv.at[pl.ds(0, pair - 1)],
        mid_ssem,
        mid_rsem,
        me,
        core,
    ).wait_recv()
    got = [mid_recv[k].astype(jnp.float32) for k in range(pair)]
    for k in range(pair):
        xf[k * whole : (k + 1) * whole, :] = got[k][:, :width]
    for n in range(packs):
        low = width + n * 128
        pack = jnp.concatenate([got[k][:, low : low + 128] for k in range(pair)], axis=0)
        spread_out = dot_f32(folding, pack.astype(jnp.bfloat16), (0, 0))
        for m in range(min(per, width // 128 - n * per)):
            lane = (n * per + m) * 128
            xf[whole * pair :, lane : lane + 128] = spread_out[
                m * pair * rest : (m + 1) * pair * rest
            ]
    mixed = norm_tokens(xf[...], params[1])
    do(PLAN[7])
    sibling_done(1)
    query, key, value = project(1, mixed)
    down, along = rows_and_columns(
        lambda n: lax.rem(n, whole), lambda n: whole + lax.rem(n, rest)
    )
    attended = attend_heads(
        query, key, value, heads_map, down == along, att, head_size, lambda head: None
    )
    final = update(1, xf[...], attended).astype(jnp.bfloat16)
    r, c = iota((tokens, 1), 0), iota((tokens, tokens), 1)
    in_half = lax.rem(r, tokens // 2)
    when_ = lax.div(r, tokens // 2) * fr_dev + lax.rem(in_half, fr_dev)
    where_ = lax.div(in_half, fr_dev)
    source = jnp.where(
        where_ < whole,
        when_ * whole + where_,
        whole * pair + when_ * rest + where_ - whole,
    )
    pick = jnp.where(c == source, 1.0, 0.0).astype(jnp.bfloat16)
    res[...] = dot_f32(pick, final, (1, 0)).astype(jnp.bfloat16).reshape(res.shape)
    fin = remote(res.at[sib], out_ref.at[core], fin_send, fin_recv, me, sib)
    fin.start()
    out_ref[core] = res[core]
    def span(layer, pieces):
        return wbuf.at[
            layer,
            pl.ds(0, pieces * piece),
            pl.ds(pl.multiple_of(core * half, 128), half),
        ]

    def drain(layer, pieces, sem):
        part = span(layer, pieces)
        remote(part, part, sem.at[layer], sib_recv.at[layer], me, sib).wait_send()

    for layer in range(layers):
        drain(layer, 15, ici_send)
        drain(layer, 3 * (count - 1), sib_send)
        when(inner == 1, lambda layer=layer: drain(layer, 10, z_send))
        when(inner == 0, lambda layer=layer: drain(layer, 2, z_send))
    remote(
        xsend.at[pl.ds(0, count - 1)], xin.at[pl.ds(0, count - 1)], in_send, in_recv, me, core
    ).wait_send()
    remote(
        mid_send.at[pl.ds(0, pair - 1)],
        mid_recv.at[pl.ds(0, pair - 1)],
        mid_ssem,
        mid_rsem,
        me,
        core,
    ).wait_send()
    fin.wait_send()
    remote(out_ref.at[sib], out_ref.at[sib], fin_send, fin_recv, me, sib).wait_recv()


def fused_device(video_tokens, timestep, w_qkv, w_out, qk_gain, mod_table, mod_gain):
    videos, fr_dev, patch_dev, width = video_tokens.shape
    layers, rows, _ = w_qkv.shape
    head_size = qk_gain.shape[2]
    feat = w_out.shape[1]
    tokens = videos * fr_dev * patch_dev
    embed = time_row(timestep, width)
    vmem = pl.BlockSpec(memory_space=pltpu.VMEM)
    hbm = pl.BlockSpec(memory_space=pl.ANY)
    count = fr_dev
    packed = width + -(-width // (1024 // (patch_dev % 8))) * 128
    bf16, f32 = jnp.bfloat16, jnp.float32
    dma = pltpu.SemaphoreType.DMA
    out = pl.pallas_call(
        functools.partial(fused_kernel, head_size),
        out_shape=jax.ShapeDtypeStruct((videos, patch_dev, fr_dev, width), bf16),
        in_specs=[vmem] * 4 + [hbm] * 3,
        out_specs=vmem,
        scratch_shapes=[
            pltpu.VMEM((layers, count * rows, 4 * feat), bf16),
            pltpu.VMEM((layers, rows, 3 * feat), bf16),
            pltpu.VMEM((layers, rows, feat), bf16),
            pltpu.VMEM((videos, patch_dev, fr_dev, width), bf16),
            pltpu.VMEM((count, videos * patch_dev, width), bf16),
            pltpu.VMEM((count, videos * patch_dev, width), bf16),
            pltpu.VMEM((2 * count, 8, packed), bf16),
            pltpu.VMEM((2 * count, 8, packed), bf16),
            pltpu.VMEM((tokens, width), f32),
            pltpu.VMEM((tokens, feat), f32),
            pltpu.VMEM((2, patch_dev, fr_dev, width), bf16),
            dma((3,)),
            dma((layers,)),
            dma((layers, 6, 4)),
            dma((layers,)),
            dma((layers,)),
            dma,
            dma,
            dma,
            dma,
            dma,
            dma,
            dma((layers,)),
        ],
        compiler_params=pltpu.CompilerParams(
            collective_id=0, has_side_effects=True, vmem_limit_bytes=56 * 1024 * 1024
        ),
        name="blocks",
    )(
        embed,
        qk_gain,
        mod_table.transpose(1, 0, 2),
        mod_gain.transpose(1, 0, 2),
        video_tokens.transpose(0, 2, 1, 3),
        w_qkv,
        w_out.transpose(0, 2, 1),
    )
    return out.transpose(0, 2, 1, 3)


def choose_device(video_tokens, timestep, w_qkv, *rest):
    videos, fr_dev, _, _ = video_tokens.shape
    fits = (videos, fr_dev) == (2, 8) and video_tokens.shape[2:] == (10, 1152) and w_qkv.shape[1] == 144
    run = fused_device if fits else per_device
    return run(video_tokens, timestep, w_qkv, *rest)


def solution(mesh):
    placed = (
        P("grp", "frame", "patch", None),
        P("grp"),
        P(None, "patch", None),
        P(None, None, "patch"),
        P(),
        P(),
        P(),
    )
    ring = (mesh.shape["grp"], mesh.shape["patch"], mesh.shape["frame"]) == (2, 8, 2)
    return jax.shard_map(
        choose_device if ring else per_device,
        mesh=mesh,
        in_specs=placed,
        out_specs=P("grp", "frame", "patch", None),
        check_vma=False,
    )
```

```python
import functools
import math

import jax
import jax.numpy as jnp
import numpy as np
from jax import lax
from jax.experimental import pallas as pl
from jax.experimental.pallas import tpu as pltpu
from jax.sharding import PartitionSpec as P


def time_embed(timestep, width):
    half_width = width // 2
    freqs = jnp.exp(-math.log(10000.0) * jnp.arange(half_width, dtype=jnp.float32) / half_width)
    angles = timestep[0].astype(jnp.float32) * freqs
    return jnp.concatenate([jnp.cos(angles), jnp.sin(angles)])


def modulate(tokens, table, gains, embed):
    params = table + gains * embed[None, :]
    values = tokens.astype(jnp.float32)
    centre = jnp.mean(values, axis=-1, keepdims=True)
    centred = values - centre
    spread = jnp.mean(centred * centred, axis=-1, keepdims=True)
    normed = centred * lax.rsqrt(spread + 1e-06)
    return ((normed * (1.0 + params[1]) + params[0]).astype(jnp.bfloat16), params[2])


def head_norm(values, gain):
    meansq = jnp.mean(values * values, axis=-1, keepdims=True)
    return (values * lax.rsqrt(meansq + 1e-06) * gain).astype(jnp.bfloat16)


def fetch_weights(qkv_rows, out_cols):
    return (
        lax.all_gather(qkv_rows, "patch", axis=0, tiled=True),
        lax.all_gather(out_cols, "patch", axis=1, tiled=True),
    )


def attend_items(stacked):
    head_size = stacked.shape[-1]
    query = stacked[0, 0]
    key = stacked[1, 0]
    value = stacked[2, 0]
    scores = jnp.einsum("nqd,nkd->nqk", query, key, preferred_element_type=jnp.float32) / math.sqrt(
        head_size
    )
    raised = jnp.exp(scores)
    total = jnp.sum(raised, axis=-1, keepdims=True)
    summed = jnp.einsum(
        "nqk,nkd->nqd", raised.astype(jnp.bfloat16), value, preferred_element_type=jnp.float32
    )
    return (summed / total).astype(jnp.bfloat16)[None]


def spatial(query, key, value, videos, fr_dev, patch_dev):
    rows, heads, head_size = query.shape
    groups = lax.axis_size("patch")
    per_group = videos * fr_dev * heads // groups
    stacked = jnp.stack([query, key, value])
    stacked = stacked.reshape(3, videos * fr_dev, patch_dev, heads, head_size)
    stacked = stacked.transpose(0, 1, 3, 2, 4).reshape(3, groups, per_group, patch_dev, head_size)
    attended = attend_items(
        lax.all_to_all(stacked, "patch", split_axis=1, concat_axis=3, tiled=True)
    )
    returned = lax.all_to_all(attended, "patch", split_axis=2, concat_axis=0, tiled=True)
    returned = returned.reshape(videos * fr_dev, heads, patch_dev, head_size).transpose(0, 2, 1, 3)
    return returned.reshape(rows, heads * head_size)


def frame_attend(query, key, value, heads):
    videos, q_frames, patches, feat = query.shape
    k_frames = key.shape[1]
    head_size = feat // heads
    query = query.reshape(videos, q_frames, patches, heads, head_size)
    key = key.reshape(videos, k_frames, patches, heads, head_size)
    value = value.reshape(videos, k_frames, patches, heads, head_size)
    scores = jnp.einsum(
        "bfphd,bgphd->bphfg", query, key, preferred_element_type=jnp.float32
    ) / math.sqrt(head_size)
    raised = jnp.exp(scores)
    total = jnp.sum(raised, axis=-1)
    summed = jnp.einsum(
        "bphfg,bgphd->bfphd", raised.astype(jnp.bfloat16), value, preferred_element_type=jnp.float32
    )
    result = summed / total.transpose(0, 3, 1, 2)[..., None]
    return result.astype(jnp.bfloat16).reshape(videos, q_frames, patches, feat)


def temporal(query, key, value, videos, fr_dev, patch_dev):
    rows, heads, head_size = query.shape
    feat = heads * head_size
    query4 = query.reshape(videos, fr_dev, patch_dev, feat)
    key4 = key.reshape(videos, fr_dev, patch_dev, feat)
    value4 = value.reshape(videos, fr_dev, patch_dev, feat)
    joined = jnp.concatenate([query4, key4, value4], axis=3)
    swapped = lax.all_to_all(joined, "frame", split_axis=2, concat_axis=1, tiled=True)
    result = frame_attend(
        swapped[..., :feat], swapped[..., feat : 2 * feat], swapped[..., 2 * feat :], heads
    )
    returned = lax.all_to_all(result, "frame", split_axis=1, concat_axis=2, tiled=True)
    return returned.reshape(rows, feat)


def per_device(video_tokens, timestep, w_qkv, w_out, qk_gain, mod_table, mod_gain):
    videos, fr_dev, patch_dev, width = video_tokens.shape
    rows = videos * fr_dev * patch_dev
    head_size = qk_gain.shape[2]
    heads = w_out.shape[1] // head_size
    embed = time_embed(timestep, width)
    tokens = video_tokens.reshape(rows, width)
    for layer in range(2):
        qkv_full, out_full = fetch_weights(w_qkv[layer], w_out[layer])
        mixed, gate = modulate(tokens, mod_table[layer], mod_gain[layer], embed)
        joint = jnp.dot(mixed, qkv_full, preferred_element_type=jnp.float32)
        joint = joint.reshape(rows, 3, heads, head_size)
        query = head_norm(joint[:, 0], qk_gain[layer, 0])
        key = head_norm(joint[:, 1], qk_gain[layer, 1])
        value = joint[:, 2].astype(jnp.bfloat16)
        if layer == 0:
            attended = spatial(query, key, value, videos, fr_dev, patch_dev)
        else:
            attended = temporal(query, key, value, videos, fr_dev, patch_dev)
        update = jnp.dot(attended, out_full, preferred_element_type=jnp.float32)
        tokens = (tokens.astype(jnp.float32) + gate * update).astype(jnp.bfloat16)
    return tokens.reshape(videos, fr_dev, patch_dev, width)


MESH = pl.DeviceIdType.MESH
HIGHEST = lax.Precision.HIGHEST


PLAN = (
    ("0a", "0s",),
    ("0z00", "1s", "0z10", "0f00", "0z01", "0f10", "0z11", "0z20", "0f20",),
    ("0x30", "1a", "1x30", "0y2", "0x00", "0f11", "0f01", "0x31", "0x10", "0z21", "1z00", "0f21", "0x20", "1z10", "0w30", "1f00", "0y0", "0w10", "1z11", "1z01", "0x11", "1f10", "0y1",),
    ("1w30", "0w00", "1z20", "0x21", "1f11", "0w20", "1f20", "0x01", "1f01", "1z21",),
    ("1x10",),
    {1: ("1f21",)},
    ("1x00", "1x31", "1w10", "1x11", "1y2", "1y0", "1y1", "1x20", "1w00", "1x21", "1x01", "1w20",),
    (),
)


def time_row(timestep, width):
    half_width = width // 2
    column = lax.broadcasted_iota(jnp.int32, (1, width), 1)
    steps = lax.rem(column, half_width).astype(jnp.float32)
    angles = timestep[0].astype(jnp.float32) * jnp.exp(-math.log(10000.0) * steps / half_width)
    return jnp.where(column < half_width, jnp.cos(angles), jnp.sin(angles))


def dot_f32(a, b, contract):
    return lax.dot_general(
        a, b, ((contract[:1], contract[1:]), ((), ())), preferred_element_type=jnp.float32
    )


def dot_exact(a, b, contract):
    return lax.dot_general(
        a,
        b,
        ((contract[:1], contract[1:]), ((), ())),
        precision=HIGHEST,
        preferred_element_type=jnp.float32,
    )


def norm_tokens(values, params):
    centre = jnp.mean(values, axis=-1, keepdims=True)
    centred = values - centre
    spread = jnp.mean(centred * centred, axis=-1, keepdims=True)
    normed = centred * lax.rsqrt(spread + 1e-06)
    return (normed * (1.0 + params[1]) + params[0]).astype(jnp.bfloat16)


def two_parts(values):
    high = values.astype(jnp.bfloat16)
    return high, (values - high.astype(jnp.float32)).astype(jnp.bfloat16)


def norm_heads(values, gain, heads_map, head_size):
    high, low = two_parts(values * values)
    total = dot_f32(high, heads_map, (1, 1)) + dot_f32(low, heads_map, (1, 1))
    scale = jnp.concatenate(two_parts(lax.rsqrt(total / head_size + 1e-06)), axis=1)
    wide = dot_f32(scale, jnp.concatenate([heads_map] * 2, axis=0), (1, 0))
    return (values * wide * gain).astype(jnp.bfloat16)


def attend_heads(query, key, value, heads_map, mask, att_ref, head_size, between):
    feat = query.shape[1]
    att_ref[...] = jnp.zeros_like(att_ref)
    for head in range(feat // head_size):
        low = head * head_size // 128 * 128
        high = min(-(-(head + 1) * head_size // 128) * 128, feat)
        lanes = heads_map[head : head + 1, low:high]
        scores = dot_f32(query[:, low:high] * lanes, key[:, low:high], (1, 1))
        raised = jnp.where(mask, jnp.exp(scores * (1.0 / math.sqrt(head_size))), 0.0)
        total = jnp.sum(raised, axis=-1, keepdims=True)
        summed = dot_f32(raised.astype(jnp.bfloat16), value[:, low:high] * lanes, (1, 0))
        att_ref[:, low:high] += summed / total
        between(head)
    return att_ref[...].astype(jnp.bfloat16)


def iota(shape, dim):
    return lax.broadcasted_iota(jnp.int32, shape, dim)


def fused_kernel(
    head_size, emb_ref, gain_ref, tab_ref, mgain_ref, x_hbm, wq_hbm, wo_hbm, out_ref,
    wbuf, stage_q, stage_o, stage_x, xsend, xin, mid_send, mid_recv, xf, att, res,
    local_sem, ici_send, ici_recv, sib_send, sib_recv,
    in_send, in_recv, mid_ssem, mid_rsem, fin_send, fin_recv, z_send,
):
    videos, patch_dev, fr_dev, width = x_hbm.shape
    layers, rows, _ = wq_hbm.shape
    feat = wo_hbm.shape[2]
    heads = feat // head_size
    count = fr_dev
    tokens = videos * patch_dev * fr_dev
    half = wbuf.shape[2] // 2
    grp = lax.axis_index("grp")
    me = lax.axis_index("patch")
    core = lax.axis_index("frame")
    sib = 1 - core
    level, side = lax.div(me, 2), lax.rem(me, 2)
    across = level * 2 + 1 - side
    piece = rows // 3
    pair = videos * count
    whole = patch_dev // 8 * 8
    rest = patch_dev - whole
    per = 8 // rest
    packs = -(-width // (128 * per))

    stage = [
        pltpu.make_async_copy(wq_hbm, stage_q, local_sem.at[0]),
        pltpu.make_async_copy(wo_hbm, stage_o, local_sem.at[1]),
        pltpu.make_async_copy(x_hbm, stage_x, local_sem.at[2]),
    ]
    for copy in stage:
        copy.start()

    barrier = pltpu.get_barrier_semaphore()
    for k in range(count):
        for s in range(2):
            if k or s:
                pl.semaphore_signal(
                    barrier,
                    inc=1,
                    device_id=(grp, lax.rem(me + k, count), lax.rem(core + s, 2)),
                    device_id_type=MESH,
                )
    pl.semaphore_signal(
        barrier, inc=1, device_id=(1 - grp, me, core), device_id_type=MESH
    )

    def remote(src, dst, send_sem, recv_sem, patch, frame, to_grp=grp):
        return pltpu.make_async_remote_copy(
            src_ref=src,
            dst_ref=dst,
            send_sem=send_sem,
            recv_sem=recv_sem,
            device_id=(to_grp, patch, frame),
            device_id_type=MESH,
        )

    def block(layer, shard, start, size, of=core):
        first = pl.multiple_of(shard * rows + start, 16)
        return wbuf.at[
            layer, pl.ds(first, size), pl.ds(pl.multiple_of(of * half, 128), half)
        ]

    def to_sibling(layer, shard, start):
        part = block(layer, shard, start, piece)
        remote(part, part, sib_send.at[layer], sib_recv.at[layer], me, sib).start()

    upper = lax.div(level, 2)
    inner = lax.rem(level + upper, 2)

    def mirrored(i):
        return (1 - upper) * i + upper * (3 - i)

    def level_of(j):
        if j == 3:
            return level
        return mirrored(j + jnp.where(j < inner, 0, 1))

    def when(cond, act):
        pl.when(cond)(act)

    start_of = (grp * 2 * piece, piece)
    lacking = ((1 - grp) * 2 * piece, piece)

    def z_to(layer, source, target, q):
        part = block(layer, source * 2 + side, start_of[q], piece)
        return remote(
            part, part, z_send.at[layer], ici_recv.at[layer, q, source], target * 2 + side, core
        )

    def x_to(layer, source, shard, q, patch):
        part = block(layer, shard, start_of[q], piece)
        return remote(
            part, part, ici_send.at[layer], ici_recv.at[layer, 2 + q, source], patch, core
        )

    def y_to(layer, kind, source, shard, start, to_grp):
        part = block(layer, shard, start, piece)
        return remote(
            part, part, ici_send.at[layer], ici_recv.at[layer, kind, source], me, core, to_grp
        )

    def send_z(layer):
        for q in range(2):
            z_to(layer, level, mirrored(1 - inner), q).start()
            when(inner == 1, lambda q=q: z_to(layer, level, mirrored(2), q).start())

    def send_x(layer):
        for q in range(2):
            x_to(layer, level, me, q, across).start()

    def pass_on(layer, j, q):
        source = level_of(j)
        shard = source * 2 + side
        x_to(layer, source, shard, q, across).start()
        if q == 0:
            y_to(layer, 4, source, shard, start_of[0], 1 - grp).start()

    def landed_z(layer, j, q):
        source = level_of(j)
        shard = source * 2 + side
        z_to(layer, source, level, q).wait_recv()
        when(
            inner == 1,
            lambda: z_to(layer, source, mirrored(2 if j == 0 else 0), q).start(),
        )
        to_sibling(layer, shard, start_of[q])

    def landed_x(layer, j, q):
        source = level_of(j)
        shard = source * 2 + 1 - side

        x_to(layer, source, shard, q, me).wait_recv()
        if q == 0:
            y_to(layer, 5, source, shard, start_of[0], 1 - grp).start()
        to_sibling(layer, shard, start_of[q])

    def landed_y(layer, j):
        source = level_of(j)
        shard = source * 2 + side
        y_to(layer, 4, source, shard, lacking[0], grp).wait_recv()
        to_sibling(layer, shard, lacking[0])

    def landed_w(layer, j, _):
        source = level_of(j)
        shard = source * 2 + 1 - side
        y_to(layer, 5, source, shard, lacking[0], grp).wait_recv()
        to_sibling(layer, shard, lacking[0])

    def do(events):
        for event in events:
            layer, kind = int(event[0]), event[1]
            args = [int(digit) for digit in event[2:]]
            actions[kind](layer, *args)

    actions = {
        "a": send_z,
        "s": send_x,
        "z": landed_z,
        "f": pass_on,
        "x": landed_x,
        "y": landed_y,
        "w": landed_w,
    }

    def sibling_done(layer):
        part = wbuf.at[
            layer,
            pl.ds(0, (count - 1) * rows),
            pl.ds(pl.multiple_of(sib * half, 128), half),
        ]
        remote(part, part, sib_send.at[layer], sib_recv.at[layer], me, sib).wait_recv()

    own_rows = pl.ds(pl.multiple_of(me * rows, 16), rows)
    stage[0].wait()
    stage[1].wait()
    for layer in range(layers):
        wbuf[layer, own_rows, : 3 * feat] = stage_q[layer]
        wbuf[layer, own_rows, 3 * feat :] = stage_o[layer]
    pl.semaphore_wait(barrier, 2 * count)
    do(PLAN[0])

    stage[2].wait()
    size = videos * patch_dev
    gap = -(-size // 8) * 8
    r, c = iota((count * gap, 1), 0), iota((count * gap, tokens), 1)
    place, frame_of = lax.rem(r, gap), lax.div(r, gap)
    after = place - videos * whole
    first = lax.div(place, whole) * patch_dev + lax.rem(place, whole)
    last = lax.div(after, rest) * patch_dev + whole + lax.rem(after, rest)
    source = jnp.where(after < 0, first, last) * fr_dev + frame_of
    pick = jnp.where((c == source) & (place < size), 1.0, 0.0).astype(jnp.bfloat16)
    moved = dot_f32(pick, stage_x[...].reshape(tokens, width), (1, 0))
    for k in range(count):
        xsend[k] = moved[k * gap : k * gap + size].astype(jnp.bfloat16)
    xin[me] = xsend[me]

    heads_map = jnp.where(
        (iota((heads, feat), 1) >= iota((heads, 1), 0) * head_size)
        & (iota((heads, feat), 1) < (iota((heads, 1), 0) + 1) * head_size),
        1.0,
        0.0,
    ).astype(jnp.bfloat16)
    spread = jnp.where(
        lax.rem(iota((head_size, feat), 1), head_size) == iota((head_size, feat), 0), 1.0, 0.0
    )
    gains = dot_exact(gain_ref[...].reshape(layers * 2, head_size), spread, (1, 0))
    params = [
        [tab_ref[i, layer : layer + 1] + mgain_ref[i, layer : layer + 1] * emb_ref[...] for i in range(3)]
        for layer in range(layers)
    ]

    def project(layer, mixed):
        joint = jnp.dot(mixed, wbuf[layer, :, : 3 * feat], preferred_element_type=jnp.float32)
        gain = gains[2 * layer : 2 * layer + 1], gains[2 * layer + 1 : 2 * layer + 2]
        query = norm_heads(joint[:, :feat], gain[0], heads_map, head_size)
        key = norm_heads(joint[:, feat : 2 * feat], gain[1], heads_map, head_size)
        return query, key, joint[:, 2 * feat :].astype(jnp.bfloat16)

    def update(layer, values, attended):
        added = dot_f32(attended, wbuf[layer, :, 3 * feat :], (1, 1))
        return values + params[layer][2] * added

    def item(r, main, left):
        return jnp.where(r < whole * pair, main(r), left(r - whole * pair))

    def rows_and_columns(main, left):
        return item(iota((tokens, 1), 0), main, left), item(iota((1, tokens), 1), main, left)

    fold = per * pair * rest
    r, c = iota((pair * 8, 1), 0), iota((pair * 8, fold), 1)
    part, within = lax.div(lax.rem(r, 8), rest), lax.rem(lax.rem(r, 8), rest)
    source = part * pair * rest + lax.div(r, 8) * rest + within
    folding = jnp.where(c == source, 1.0, 0.0).astype(jnp.bfloat16)

    do(PLAN[1])
    for k in range(1, count):
        peer = lax.rem(me + k, count)
        remote(xsend.at[peer], xin.at[me], in_send, in_recv, peer, core).start()
    do(PLAN[2])
    remote(
        xsend.at[pl.ds(0, count - 1)], xin.at[pl.ds(0, count - 1)], in_send, in_recv, me, core
    ).wait_recv()
    for k in range(count):
        got = xin[k].astype(jnp.float32)
        low, step = k * videos * whole, videos * rest
        xf[low : low + videos * whole, :] = got[: videos * whole]
        low = pair * whole + k * step
        xf[low : low + step, :] = got[videos * whole :]
    mixed = norm_tokens(xf[...], params[0])
    do(PLAN[3])
    sibling_done(0)
    do(PLAN[4])
    query, key, value = project(0, mixed)
    down, along = rows_and_columns(
        lambda n: lax.rem(lax.div(n, whole), videos), lambda n: lax.rem(lax.div(n, rest), videos)
    )
    attended = attend_heads(
        query, key, value, heads_map, down == along, att, head_size,
        lambda head: do(PLAN[5].get(head, ())),
    )
    done = update(0, xf[...], attended).astype(jnp.bfloat16)

    frame = core * count + me
    left = done[whole * pair :]
    lanes = [left[:, low : low + 128] for low in range(0, width, 128)]
    lanes += [jnp.zeros_like(lanes[0])] * (packs * per - len(lanes))
    packed = [
        dot_f32(folding, jnp.concatenate(lanes[n * per : (n + 1) * per], axis=0), (1, 0))
        for n in range(packs)
    ]
    full = done[: whole * pair].astype(jnp.float32)
    for k in range(pair):
        rows_k = slice(k * whole, (k + 1) * whole)
        mid_send[k, :, :width] = full[rows_k].astype(jnp.bfloat16)
        for n in range(packs):
            low = width + n * 128
            mid_send[k, :, low : low + 128] = packed[n][k * 8 : k * 8 + 8].astype(jnp.bfloat16)
    for s in range(2):
        for k in range(count):
            if k or s:
                peer, video = lax.rem(me + k, count), lax.rem(core + s, 2)
                remote(
                    mid_send.at[peer * videos + video],
                    mid_recv.at[frame],
                    mid_ssem,
                    mid_rsem,
                    peer,
                    video,
                ).start()
    mid_recv[frame] = mid_send[me * videos + core]
    def rows_of(frames):
        r, c = iota((tokens // 2, 1), 0), iota((tokens // 2, tokens), 1)
        when_, where_ = frames * fr_dev + lax.rem(r, fr_dev), lax.div(r, fr_dev)
        source = jnp.where(
            where_ < whole,
            when_ * whole + where_,
            whole * pair + when_ * rest + where_ - whole,
        )
        return jnp.where(c == source, 1.0, 0.0).astype(jnp.bfloat16)

    pick_sib, pick_own = rows_of(sib), rows_of(core)
    do(PLAN[6])
    remote(
        mid_send.at[pl.ds(0, pair - 1)],
        mid_recv.at[pl.ds(0, pair - 1)],
        mid_ssem,
        mid_rsem,
        me,
        core,
    ).wait_recv()
    got = [mid_recv[k].astype(jnp.float32) for k in range(pair)]
    for k in range(pair):
        xf[k * whole : (k + 1) * whole, :] = got[k][:, :width]
    for n in range(packs):
        low = width + n * 128
        pack = jnp.concatenate([got[k][:, low : low + 128] for k in range(pair)], axis=0)
        spread_out = dot_f32(folding, pack.astype(jnp.bfloat16), (0, 0))
        for m in range(min(per, width // 128 - n * per)):
            lane = (n * per + m) * 128
            xf[whole * pair :, lane : lane + 128] = spread_out[
                m * pair * rest : (m + 1) * pair * rest
            ]
    mixed = norm_tokens(xf[...], params[1])
    do(PLAN[7])
    sibling_done(1)
    query, key, value = project(1, mixed)
    down, along = rows_and_columns(
        lambda n: lax.rem(n, whole), lambda n: whole + lax.rem(n, rest)
    )
    attended = attend_heads(
        query, key, value, heads_map, down == along, att, head_size, lambda head: None
    )
    final = update(1, xf[...], attended).astype(jnp.bfloat16)
    res[sib] = dot_f32(pick_sib, final, (1, 0)).astype(jnp.bfloat16).reshape(res.shape[1:])
    fin = remote(res.at[sib], out_ref.at[core], fin_send, fin_recv, me, sib)
    fin.start()
    own = dot_f32(pick_own, final, (1, 0))
    out_ref[core] = own.astype(jnp.bfloat16).reshape(res.shape[1:])
    def span(layer, pieces):
        return wbuf.at[
            layer,
            pl.ds(0, pieces * piece),
            pl.ds(pl.multiple_of(core * half, 128), half),
        ]

    def drain(layer, pieces, sem):
        part = span(layer, pieces)
        remote(part, part, sem.at[layer], sib_recv.at[layer], me, sib).wait_send()

    for layer in range(layers):
        drain(layer, 15, ici_send)
        drain(layer, 3 * (count - 1), sib_send)
        when(inner == 1, lambda layer=layer: drain(layer, 10, z_send))
        when(inner == 0, lambda layer=layer: drain(layer, 2, z_send))
    remote(
        xsend.at[pl.ds(0, count - 1)], xin.at[pl.ds(0, count - 1)], in_send, in_recv, me, core
    ).wait_send()
    remote(
        mid_send.at[pl.ds(0, pair - 1)],
        mid_recv.at[pl.ds(0, pair - 1)],
        mid_ssem,
        mid_rsem,
        me,
        core,
    ).wait_send()
    fin.wait_send()
    remote(out_ref.at[sib], out_ref.at[sib], fin_send, fin_recv, me, sib).wait_recv()


def fused_device(video_tokens, timestep, w_qkv, w_out, qk_gain, mod_table, mod_gain):
    videos, fr_dev, patch_dev, width = video_tokens.shape
    layers, rows, _ = w_qkv.shape
    head_size = qk_gain.shape[2]
    feat = w_out.shape[1]
    tokens = videos * fr_dev * patch_dev
    embed = time_row(timestep, width)
    vmem = pl.BlockSpec(memory_space=pltpu.VMEM)
    hbm = pl.BlockSpec(memory_space=pl.ANY)
    count = fr_dev
    packed = width + -(-width // (1024 // (patch_dev % 8))) * 128
    bf16, f32 = jnp.bfloat16, jnp.float32
    dma = pltpu.SemaphoreType.DMA
    out = pl.pallas_call(
        functools.partial(fused_kernel, head_size),
        out_shape=jax.ShapeDtypeStruct((videos, patch_dev, fr_dev, width), bf16),
        in_specs=[vmem] * 4 + [hbm] * 3,
        out_specs=vmem,
        scratch_shapes=[
            pltpu.VMEM((layers, count * rows, 4 * feat), bf16),
            pltpu.VMEM((layers, rows, 3 * feat), bf16),
            pltpu.VMEM((layers, rows, feat), bf16),
            pltpu.VMEM((videos, patch_dev, fr_dev, width), bf16),
            pltpu.VMEM((count, videos * patch_dev, width), bf16),
            pltpu.VMEM((count, videos * patch_dev, width), bf16),
            pltpu.VMEM((2 * count, 8, packed), bf16),
            pltpu.VMEM((2 * count, 8, packed), bf16),
            pltpu.VMEM((tokens, width), f32),
            pltpu.VMEM((tokens, feat), f32),
            pltpu.VMEM((2, patch_dev, fr_dev, width), bf16),
            dma((3,)),
            dma((layers,)),
            dma((layers, 6, 4)),
            dma((layers,)),
            dma((layers,)),
            dma,
            dma,
            dma,
            dma,
            dma,
            dma,
            dma((layers,)),
        ],
        compiler_params=pltpu.CompilerParams(
            collective_id=0, has_side_effects=True, vmem_limit_bytes=56 * 1024 * 1024
        ),
        name="blocks",
    )(
        embed,
        qk_gain,
        mod_table.transpose(1, 0, 2),
        mod_gain.transpose(1, 0, 2),
        video_tokens.transpose(0, 2, 1, 3),
        w_qkv,
        w_out.transpose(0, 2, 1),
    )
    return out.transpose(0, 2, 1, 3)


def choose_device(video_tokens, timestep, w_qkv, *rest):
    videos, fr_dev, _, _ = video_tokens.shape
    fits = (videos, fr_dev) == (2, 8) and video_tokens.shape[2:] == (10, 1152) and w_qkv.shape[1] == 144
    run = fused_device if fits else per_device
    return run(video_tokens, timestep, w_qkv, *rest)


def solution(mesh):
    placed = (
        P("grp", "frame", "patch", None),
        P("grp"),
        P(None, "patch", None),
        P(None, None, "patch"),
        P(),
        P(),
        P(),
    )
    ring = (mesh.shape["grp"], mesh.shape["patch"], mesh.shape["frame"]) == (2, 8, 2)
    return jax.shard_map(
        choose_device if ring else per_device,
        mesh=mesh,
        in_specs=placed,
        out_specs=P("grp", "frame", "patch", None),
        check_vma=False,
    )
```
